512 devices in a mesh: cls: 64 (over x, z, y_hi), dp: 8 (over y_lo, core).
Axes of the slice: x: 4, y: 8 (y_hi: 2, y_lo: 4; y = y_hi * 4 + y_lo), z: 8, core: 2. Of those that a mesh axis runs over, the one named last changes fastest.
Arguments:
- features: bfloat16 [65536, 512], P(('cls', 'dp')), may hold values from -6 to 6
- labels: int32 [65536], P(('cls', 'dp')), may hold values from 0 to 16383, as said below
- weights: float32 [65536, 512], P('cls'), may hold values from -0.25 to 0.25
- sampled: int32 [16384], P('cls'), may hold values from 0 to 1023, as said below
Outputs:
- sample_loss: float32 [65536], P(('cls', 'dp'))
- weight_grad: float32 [16384, 512], P(('cls', 'dp'))
The draws below stay inside these ranges and needn't reach their ends.
Inputs may be any that keep to these rules, and one draw needn't show every extreme that they name: The owner of a label is label // 256. In the rows of one device (aligned blocks of 128 rows) exactly one owner receives 4 of the labels and every other owner fewer. `sampled`: each aligned block of 256 entries holds distinct rows of the owner's bank.
All inputs are finite; a program needn't handle non-finite values.
Results may differ from the reference program's by a relative error of at most 0.0038.
Values may be sent and summed in bfloat16 or wider, within the bound.
A program may use at most 64 MiB of HBM per device.

```python
import math
import jax
import jax.numpy as jnp
from jax import lax

D = 512
B_DEV = 128
BANK = 1024
SAMP = 256
CAP = 4
BATCH = 65536
BANK_ALL = 65536
SAMPLED_ALL = 16384
N_CLS = 64
N_DP = 8


def draw_sampled(key, part):
    keys = jax.random.split(key, N_CLS)

    def one_shard(shard_key):
        return jax.random.permutation(shard_key, BANK)[:SAMP]
    picked = jax.vmap(one_shard)(keys)
    return picked.reshape(-1).astype(jnp.int32)


def draw_labels(key, part):
    count_blocks = BATCH // B_DEV
    keys = jax.random.split(key, count_blocks)

    def one_block(block_key):
        key_hot, key_rest, key_order, key_slot = jax.random.split(block_key, 4)
        hot_owner = jax.random.randint(key_hot, (), 0, N_CLS).astype(jnp.int32)
        candidates = jnp.repeat(jnp.arange(N_CLS - 1, dtype=jnp.int32), CAP - 1)
        others = jax.random.permutation(key_rest, candidates)[:B_DEV - CAP]
        others = others + (others >= hot_owner).astype(jnp.int32)
        owner_ids = jnp.concatenate([jnp.full((CAP,), hot_owner, jnp.int32), others])
        owner_ids = jax.random.permutation(key_order, owner_ids)
        slot_ids = jax.random.randint(key_slot, (B_DEV,), 0, SAMP).astype(jnp.int32)
        return owner_ids * SAMP + slot_ids
    return jax.vmap(one_block)(keys).reshape(-1).astype(jnp.int32)


def block_scale(key, shape, cuts, least, high):
    loudness, own = 1.0, jax.random.fold_in(key, 6)
    for position, parts in cuts:
        steps = jnp.exp(jax.random.uniform(jax.random.fold_in(own, position), (parts,), jnp.float32, least / len(cuts), high / len(cuts)))
        loudness = loudness * jnp.repeat(steps, shape[position] // parts).reshape([-1 if axis == position else 1 for axis in range(len(shape))])
    return loudness


def gaussian(rng, dims, deviation, bound, cuts=(), kind=jnp.bfloat16):
    result = jax.random.normal(rng, dims, jnp.float32) * deviation
    if len(cuts) > 0:
        result = block_scale(rng, dims, cuts, -0.22, 0.18) * result
    return jnp.clip(result, min=-bound, max=bound).astype(kind)


def setup_inputs(seed: int = 0) -> dict:
    key_of = jax.random.split(jax.random.key(seed), 5)
    features = gaussian(key_of[0], (BATCH, D), 1.0, 6.0, ((0, 512),))
    labels = draw_labels(jax.random.fold_in(key_of[4], 71), 0)
    weights = gaussian(key_of[2], (BANK_ALL, D), D ** -0.5, 0.25, ((0, 64),), jnp.float32)
    sampled = draw_sampled(jax.random.fold_in(key_of[4], 71), 0)
    return dict(features=features, labels=labels, weights=weights, sampled=sampled)


logit_scale = 64.0
margin = 0.35
epsilon = 1e-06

def normalize_rows(matrix):
    squares = lax.optimization_barrier(jnp.sum(matrix * matrix, axis=1, keepdims=True))
    return lax.rsqrt(squares + epsilon)

def reference(features, labels, weights, sampled):
    feat_wide = features.astype(jnp.float32)
    unit_feats = (feat_wide * normalize_rows(feat_wide)).astype(jnp.bfloat16)
    bank_rows = sampled + jnp.arange(SAMPLED_ALL, dtype=jnp.int32) // SAMP * BANK
    chosen = weights[bank_rows]
    inverse_norm = normalize_rows(chosen)
    unit_f32 = chosen * inverse_norm
    unit_rows = unit_f32.astype(jnp.bfloat16)
    class_ids = jnp.arange(SAMPLED_ALL, dtype=jnp.int32)
    block_rows = math.gcd(BATCH, 512)
    feat_blocks = unit_feats.reshape(BATCH // block_rows, block_rows, D)
    label_blocks = labels.reshape(BATCH // block_rows, block_rows)

    def logits_of(feat_block, label_block):
        cosine = jnp.dot(feat_block, unit_rows.T, preferred_element_type=jnp.float32)
        target_hit = label_block[:, None] == class_ids[None, :]
        logits = logit_scale * (cosine - margin * target_hit.astype(jnp.float32))
        return (logits, target_hit)

    def first_pass(operands):
        logits, target_hit = logits_of(operands[0], operands[1])
        totals = lax.optimization_barrier(jnp.sum(jnp.exp(logits - logit_scale), axis=1))
        targets = lax.optimization_barrier(jnp.sum(jnp.where(target_hit, logits, 0.0), axis=1))
        return (totals, targets)
    totals, targets = lax.map(first_pass, (feat_blocks, label_blocks))
    sample_loss = logit_scale + jnp.log(totals) - targets

    def second_pass(running, triple):
        logits, target_hit = logits_of(triple[0], triple[1])
        softmax = jnp.exp(logits - logit_scale) / triple[2][:, None]
        grads_low = (logit_scale * (softmax - target_hit.astype(jnp.float32)) / N_DP).astype(jnp.bfloat16)
        return (running + jnp.dot(grads_low.T, triple[0], preferred_element_type=jnp.float32), None)
    start_grad = jnp.zeros((SAMPLED_ALL, D), jnp.float32)
    unit_grad, _ = lax.scan(second_pass, start_grad, (feat_blocks, label_blocks, totals))
    radial = lax.optimization_barrier(jnp.sum(unit_f32 * unit_grad, axis=1, keepdims=True))
    weight_grad = inverse_norm * (unit_grad - unit_f32 * radial)
    return (sample_loss.reshape(BATCH), weight_grad)
```

```python
import functools

import jax
import jax.numpy as jnp
from jax import lax
from jax.experimental import pallas as pl
from jax.experimental.pallas import tpu as pltpu
from jax.sharding import PartitionSpec as P

logit_scale = 64.0
margin = 0.35
epsilon = 1e-06

NX, NZ, NYH, NYL, NCORE = 4, 8, 2, 4, 2
ROWS = 128
OUT_ROWS = 32
WIDTH = 512
PAIR = 2 * ROWS


def normalize_rows(matrix):
    squares = jnp.sum(matrix * matrix, axis=1, keepdims=True)
    return lax.rsqrt(squares + epsilon)


def head_kernel(
    feat_ref,
    label_ref,
    class_ref,
    unit_ref,
    inverse_ref,
    loss_ref,
    grad_ref,
    feats,
    classes,
    labels,
    ids,
    probs,
    grads,
    inverse_total,
    sums,
    sums_in,
    targets,
    targets_in,
    part_out,
    part_in,
    part_own,
    half_out,
    half_own,
    half_in,
    feat_send,
    feat_recv,
    core_send,
    core_recv,
    label_send,
    label_recv,
    class_send,
    class_recv,
    sum_send,
    sum_recv,
    target_send,
    target_recv,
    part_send,
    part_recv,
    half_send,
    half_recv,
):
    cls, dp = lax.axis_index("cls"), lax.axis_index("dp")
    x, z, yh = lax.div(cls, 16), lax.rem(lax.div(cls, 2), 8), lax.rem(cls, 2)
    yl, core = lax.div(dp, 2), lax.rem(dp, 2)

    def device(dx=0, dz=0, dyh=0, dyl=0, dcore=0):
        px = lax.rem(x + dx, NX)
        pz = lax.rem(z + dz, NZ)
        pyh = lax.rem(yh + dyh, NYH)
        pyl = lax.rem(yl + dyl, NYL)
        pcore = lax.rem(core + dcore, NCORE)
        return ((px * NZ + pz) * NYH + pyh, pyl * NCORE + pcore)

    mirror = ((x * NZ + z) * NYH + (1 - yh), (NYL - 1 - yl) * NCORE + core)

    def copy(src, dst, send, recv, target):
        return pltpu.make_async_remote_copy(
            src_ref=src,
            dst_ref=dst,
            send_sem=send,
            recv_sem=recv,
            device_id=target,
            device_id_type=pl.DeviceIdType.MESH,
        )

    plane = [(o, w) for o in range(NZ) for w in range(NCORE) if (o, w) != (0, 0)]
    column = [(u, v) for u in range(NYH) for v in range(NYL) if (u, v) != (0, 0)]

    barrier = pltpu.get_barrier_semaphore()
    peers = [device(dz=o, dcore=w) for o, w in plane]
    peers += [device(dx=i) for i in range(1, NX)]
    peers += [device(dyh=u, dyl=v) for u, v in column]
    for peer in peers:
        pl.semaphore_signal(barrier, inc=1, device_id=peer, device_id_type=pl.DeviceIdType.MESH)
    pl.semaphore_wait(barrier, len(peers))

    def feat_copy(slot):
        if slot <= NZ // 2:
            came, target = slot - 1, device(dz=1)
        else:
            came, target = (slot + 1) % NZ, device(dz=NZ - 1)
        src = feat_ref if came == 0 else feats.at[came, pl.ds(0, ROWS)]
        return copy(
            src, feats.at[slot, pl.ds(0, ROWS)], feat_send.at[slot], feat_recv.at[slot], target
        )

    def core_copy(slot):
        src = feat_ref if slot == 0 else feats.at[slot, pl.ds(0, ROWS)]
        return copy(
            src,
            feats.at[slot, pl.ds(ROWS, ROWS)],
            core_send.at[slot],
            core_recv.at[slot],
            device(dcore=1),
        )

    def class_copy(i, u):
        if i == 0:
            src, target = class_ref, mirror
        else:
            src = class_ref if u == 0 else classes.at[0, pl.ds(ROWS, ROWS)]
            target = device(dx=i)
        k = 2 * i + u
        return copy(
            src, classes.at[i, pl.ds(u * ROWS, ROWS)], class_send.at[k], class_recv.at[k], target
        )

    def label_copy(o, w):
        k = 2 * o + w
        return copy(
            label_ref, labels.at[k], label_send.at[k], label_recv.at[k], device(dz=o, dcore=w)
        )

    feat_copies = {s: feat_copy(s) for s in range(1, NZ)}
    core_copies = {s: core_copy(s) for s in range(NZ)}
    class_copies = {(i, u): class_copy(i, u) for i in range(NX) for u in range(2) if i + u}
    label_copies = [label_copy(o, w) for o, w in plane]

    class_copies[0, 1].start()
    feat_copies[1].start()
    feat_copies[NZ - 1].start()
    for i in (2, 1, 3):
        class_copies[i, 0].start()
    core_copies[0].start()
    for one in label_copies:
        one.start()

    feats[0, :ROWS] = feat_ref[...]
    classes[0, :ROWS] = class_ref[...]
    labels[0] = label_ref[...]
    row = lax.broadcasted_iota(jnp.int32, (PAIR, PAIR), 0)
    upper = row >= ROWS
    within = jnp.where(upper, row - ROWS, row)
    ids[...] = (
        z * (2 * PAIR)
        + jnp.where(upper, (1 - yh) * PAIR, yh * PAIR)
        + lax.shift_right_logical(within, 5) * (2 * OUT_ROWS)
        + core * OUT_ROWS
        + lax.bitwise_and(within, OUT_ROWS - 1)
    )

    for step in range(1, NZ // 2 + 1):
        feat_copies[step].wait_recv()
        if step < NZ // 2:
            feat_copies[step + 1].start()
        core_copies[step].start()
        if step < NZ // 2:
            feat_copies[NZ - step].wait_recv()
            if step < NZ // 2 - 1:
                feat_copies[NZ - step - 1].start()
            core_copies[NZ - step].start()
        if step == 1:
            class_copies[0, 1].wait_recv()
            for i in (2, 1, 3):
                class_copies[i, 1].start()

    for one in label_copies:
        one.wait_recv()
    for one in core_copies.values():
        one.wait_recv()
    for key, one in class_copies.items():
        if key != (0, 1):
            one.wait_recv()

    def hits(s, i):
        names = jnp.concatenate([labels[2 * s], labels[2 * s + 1]], axis=1)
        bank = lax.rem(x + (NX - i), NX) * (NZ * NYH * PAIR)
        return ids[...] == names - bank

    def first_pass(s, carry):
        block = feats[s]
        total = jnp.zeros((1, PAIR), jnp.float32)
        target = jnp.zeros((1, PAIR), jnp.float32)
        for i in range(NX):
            cosine = lax.dot_general(
                classes[i],
                block,
                (((1,), (1,)), ((), ())),
                preferred_element_type=jnp.float32,
            )
            hit = hits(s, i)
            logits = logit_scale * (cosine - jnp.where(hit, margin, 0.0))
            prob = jnp.exp(logits - logit_scale)
            probs[i, s] = prob
            total += jnp.sum(prob, axis=0, keepdims=True)
            target += jnp.sum(jnp.where(hit, logits, 0.0), axis=0, keepdims=True)
        sums[0, pl.ds(s, 1)] = total[:, :ROWS]
        sums[1, pl.ds(s, 1)] = total[:, ROWS:]
        targets[2 * s] = target[:, :ROWS]
        targets[2 * s + 1] = target[:, ROWS:]
        return carry

    lax.fori_loop(0, NZ, first_pass, 0)

    sum_copies, target_copies = {}, {}
    for o, w in plane:
        k = 2 * o + w
        sum_copies[o, w] = copy(
            sums, sums_in.at[k], sum_send.at[k], sum_recv.at[k], device(dz=o, dcore=w)
        )
        target_copies[o, w] = copy(
            targets.at[k],
            targets_in.at[k],
            target_send.at[k],
            target_recv.at[k],
            device(dz=NZ - o, dcore=w),
        )
    for one in sum_copies.values():
        one.start()
    for one in target_copies.values():
        one.start()
    whole = [sums[0], sums[1]]
    for (o, w), one in sum_copies.items():
        one.wait_recv()
        for q in range(2):
            other = sums_in[2 * o + w, (q + w) % 2]
            whole[q] += other if o == 0 else pltpu.roll(other, o, 0)
    for q in range(2):
        inverse_total[q] = 1.0 / whole[q]

    part_copies = {}
    for i in (2, 1, 3, 0):

        def weigh(s, carry):
            inverse = jnp.concatenate(
                [inverse_total[0, pl.ds(s, 1)], inverse_total[1, pl.ds(s, 1)]], axis=1
            )
            hit = hits(s, i)
            slope = (logit_scale / 8.0) * (probs[i, s] * inverse - jnp.where(hit, 1.0, 0.0))
            grads[s] = slope.astype(jnp.bfloat16)
            return carry

        lax.fori_loop(0, NZ, weigh, 0)
        part = jnp.zeros((PAIR, WIDTH), jnp.float32)
        for s in range(NZ):
            part += jnp.dot(grads[s], feats[s], preferred_element_type=jnp.float32)
        if i == 0:
            part_own[...] = part
        else:
            part_out[i] = part.astype(jnp.bfloat16)
            part_copies[i] = copy(
                part_out.at[i],
                part_in.at[i],
                part_send.at[i],
                part_recv.at[i],
                device(dx=NX - i),
            )
            part_copies[i].start()

    own_target = targets[0]
    for (o, w), one in target_copies.items():
        one.wait_recv()
        own_target += targets_in[2 * o + w]
    loss_ref[...] = logit_scale + jnp.log(whole[0][0:1]) - own_target

    half = part_own[...]
    for i in (1, 3, 2):
        part_copies[i].wait_recv()
        half += part_in[i].astype(jnp.float32)
    half = half.reshape(NYH * NYL, OUT_ROWS, WIDTH)
    half_own[...] = half
    half_out[...] = half.astype(jnp.bfloat16)
    half_copies = {}
    for u, v in column:
        k = NYL * u + v
        half_copies[u, v] = copy(
            half_out.at[NYL * u + lax.rem(yl + v, NYL)],
            half_in.at[k],
            half_send.at[k],
            half_recv.at[k],
            device(dyh=u, dyl=v),
        )
        half_copies[u, v].start()
    total = half_own[yl]
    for (u, v), one in half_copies.items():
        one.wait_recv()
        total += half_in[NYL * u + v].astype(jnp.float32)
    unit = unit_ref[...]
    radial = jnp.sum(unit * total, axis=1, keepdims=True)
    grad_ref[...] = inverse_ref[...] * (total - unit * radial)

    for group in (
        feat_copies,
        core_copies,
        class_copies,
        sum_copies,
        target_copies,
        part_copies,
        half_copies,
    ):
        for one in group.values():
            one.wait_send()
    for one in label_copies:
        one.wait_send()


def head(unit_feats, labels, class_rows, unit_own, inverse_own):
    vmem = pl.BlockSpec(memory_space=pltpu.VMEM)
    dma = pltpu.SemaphoreType.DMA
    slots = NZ * NCORE
    scratch = [
        pltpu.VMEM((NZ, PAIR, WIDTH), jnp.bfloat16),
        pltpu.VMEM((NX, PAIR, WIDTH), jnp.bfloat16),
        pltpu.VMEM((slots, 1, ROWS), jnp.int32),
        pltpu.VMEM((PAIR, PAIR), jnp.int32),
        pltpu.VMEM((NX, NZ, PAIR, PAIR), jnp.float32),
        pltpu.VMEM((NZ, PAIR, PAIR), jnp.bfloat16),
        pltpu.VMEM((2, NZ, ROWS), jnp.float32),
        pltpu.VMEM((2, NZ, ROWS), jnp.float32),
        pltpu.VMEM((slots, 2, NZ, ROWS), jnp.float32),
        pltpu.VMEM((slots, 1, ROWS), jnp.float32),
        pltpu.VMEM((slots, 1, ROWS), jnp.float32),
        pltpu.VMEM((NX, PAIR, WIDTH), jnp.bfloat16),
        pltpu.VMEM((NX, PAIR, WIDTH), jnp.bfloat16),
        pltpu.VMEM((PAIR, WIDTH), jnp.float32),
        pltpu.VMEM((NYH * NYL, OUT_ROWS, WIDTH), jnp.bfloat16),
        pltpu.VMEM((NYH * NYL, OUT_ROWS, WIDTH), jnp.float32),
        pltpu.VMEM((NYH * NYL, OUT_ROWS, WIDTH), jnp.bfloat16),
    ]
    for count in (NZ, NZ, slots, 2 * NX, slots, slots, NX, NYH * NYL):
        scratch += [dma((count,)), dma((count,))]
    return pl.pallas_call(
        head_kernel,
        out_shape=(
            jax.ShapeDtypeStruct((1, ROWS), jnp.float32),
            jax.ShapeDtypeStruct((OUT_ROWS, WIDTH), jnp.float32),
        ),
        in_specs=[vmem] * 5,
        out_specs=(vmem, vmem),
        scratch_shapes=scratch,
        compiler_params=pltpu.CompilerParams(
            collective_id=0, has_side_effects=True, vmem_limit_bytes=48 * 1024 * 1024
        ),
    )(unit_feats, labels, class_rows, unit_own, inverse_own)


def per_device(features, labels, weights, sampled):
    dp = lax.axis_index("dp")
    core, yl = dp % NCORE, dp // NCORE
    feat_wide = features.astype(jnp.float32)
    unit_feats = (feat_wide * normalize_rows(feat_wide)).astype(jnp.bfloat16)
    picked = lax.dynamic_index_in_dim(
        sampled.reshape(NYL, NCORE, OUT_ROWS), core, axis=1, keepdims=False
    ).reshape(ROWS)
    chosen = weights[picked]
    inverse_norm = normalize_rows(chosen)
    unit_f32 = chosen * inverse_norm
    unit_own = lax.dynamic_slice_in_dim(unit_f32, yl * OUT_ROWS, OUT_ROWS)
    inverse_own = lax.dynamic_slice_in_dim(inverse_norm, yl * OUT_ROWS, OUT_ROWS)
    loss, grad = head(
        unit_feats,
        labels.reshape(1, ROWS),
        unit_f32.astype(jnp.bfloat16),
        unit_own,
        inverse_own,
    )
    return (loss.reshape(ROWS), grad)


def solution(mesh):
    in_specs = (P(("cls", "dp"), None), P(("cls", "dp")), P("cls", None), P("cls"))
    out_specs = (P(("cls", "dp")), P(("cls", "dp"), None))
    return jax.shard_map(
        per_device, mesh=mesh, in_specs=in_specs, out_specs=out_specs, check_vma=False
    )
```

```python
import functools

import jax
import jax.numpy as jnp
from jax import lax
from jax.experimental import pallas as pl
from jax.experimental.pallas import tpu as pltpu
from jax.sharding import PartitionSpec as P

logit_scale = 64.0
margin = 0.35
epsilon = 1e-06

NX, NZ, NYH, NYL, NCORE = 4, 8, 2, 4, 2
ROWS = 128
OUT_ROWS = 32
WIDTH = 512
PAIR = 2 * ROWS
HALF = ROWS // 2
BANKS = NX * ROWS
EAST = 384
NORTH = WIDTH - EAST


def normalize_rows(matrix):
    squares = jnp.sum(matrix * matrix, axis=1, keepdims=True)
    return lax.rsqrt(squares + epsilon)


def head_kernel(
    feat_ref,
    label_ref,
    class_ref,
    unit_ref,
    inverse_ref,
    loss_ref,
    grad_ref,
    feats,
    classes,
    labels,
    ids,
    probs,
    grads,
    inverse_total,
    sums,
    sums_in,
    targets,
    targets_in,
    part_out,
    part_in,
    part_own,
    half_out,
    half_own,
    half_in,
    north_out,
    north_own,
    north_in,
    last_out,
    last_in,
    feat_send,
    feat_recv,
    core_send,
    core_recv,
    label_send,
    label_recv,
    class_send,
    class_recv,
    sum_send,
    sum_recv,
    target_send,
    target_recv,
    part_send,
    part_recv,
    half_send,
    half_recv,
    north_send,
    north_recv,
    last_send,
    last_recv,
):
    cls, dp = lax.axis_index("cls"), lax.axis_index("dp")
    x, z, yh = lax.div(cls, 16), lax.rem(lax.div(cls, 2), 8), lax.rem(cls, 2)
    yl, core = lax.div(dp, 2), lax.rem(dp, 2)

    def device(dx=0, dz=0, dyh=0, dyl=0, dcore=0):
        px = lax.rem(x + dx, NX)
        pz = lax.rem(z + dz, NZ)
        pyh = lax.rem(yh + dyh, NYH)
        pyl = lax.rem(yl + dyl, NYL)
        pcore = lax.rem(core + dcore, NCORE)
        return ((px * NZ + pz) * NYH + pyh, pyl * NCORE + pcore)

    mirror = ((x * NZ + z) * NYH + (1 - yh), (NYL - 1 - yl) * NCORE + core)

    def copy(src, dst, send, recv, target):
        return pltpu.make_async_remote_copy(
            src_ref=src,
            dst_ref=dst,
            send_sem=send,
            recv_sem=recv,
            device_id=target,
            device_id_type=pl.DeviceIdType.MESH,
        )

    plane = [(o, w) for o in range(NZ) for w in range(NCORE) if (o, w) != (0, 0)]
    column = [(u, v) for u in range(NYH) for v in range(NYL) if (u, v) != (0, 0)]

    barrier = pltpu.get_barrier_semaphore()
    peers = [device(dz=o, dcore=w) for o, w in plane]
    peers += [device(dx=i) for i in range(1, NX)]
    peers += [device(dyh=u, dyl=v) for u, v in column]
    for peer in peers:
        pl.semaphore_signal(barrier, inc=1, device_id=peer, device_id_type=pl.DeviceIdType.MESH)
    pl.semaphore_wait(barrier, len(peers))

    def feat_copy(slot, h):
        if slot <= NZ // 2:
            came, target = slot - 1, device(dz=1)
        else:
            came, target = (slot + 1) % NZ, device(dz=NZ - 1)
        rows = pl.ds(h * HALF, HALF)
        src = feat_ref.at[rows] if came == 0 else feats.at[came, rows]
        k = 2 * slot + h
        return copy(src, feats.at[slot, rows], feat_send.at[k], feat_recv.at[k], target)

    def core_copy(slot, h):
        rows = pl.ds(h * HALF, HALF)
        src = feat_ref.at[rows] if slot == 0 else feats.at[slot, rows]
        k = 2 * slot + h
        return copy(
            src,
            feats.at[slot, pl.ds(ROWS + h * HALF, HALF)],
            core_send.at[k],
            core_recv.at[k],
            device(dcore=1),
        )

    def class_copy(i, u, h):
        rows = pl.ds(i * ROWS + h * HALF, HALF)
        near = pl.ds(h * HALF, HALF)
        if i == 0:
            src, target = class_ref.at[near], mirror
        else:
            src = class_ref.at[near] if u == 0 else classes.at[1, near]
            target = device(dx=i)
        k = 4 * i + 2 * u + h
        return copy(src, classes.at[u, rows], class_send.at[k], class_recv.at[k], target)

    def label_copy(o, w):
        k = 2 * o + w
        return copy(
            label_ref, labels.at[k], label_send.at[k], label_recv.at[k], device(dz=o, dcore=w)
        )

    feat_copies = {(s, h): feat_copy(s, h) for s in range(1, NZ) for h in range(2)}
    core_copies = {(s, h): core_copy(s, h) for s in range(NZ) for h in range(2)}
    class_copies = {
        (i, u, h): class_copy(i, u, h)
        for i in range(NX)
        for u in range(2)
        for h in range(2)
        if i + u
    }
    label_copies = [label_copy(o, w) for o, w in plane]

    for h in range(2):
        class_copies[0, 1, h].start()
        feat_copies[1, h].start()
        feat_copies[NZ - 1, h].start()
    for i in (2, 1, 3):
        for h in range(2):
            class_copies[i, 0, h].start()
    for h in range(2):
        core_copies[0, h].start()
    for one in label_copies:
        one.start()

    feats[0, :ROWS] = feat_ref[...]
    classes[0, :ROWS] = class_ref[...]
    labels[0] = label_ref[...]
    sums[...] = jnp.zeros_like(sums)
    targets[...] = jnp.zeros_like(targets)
    row = lax.broadcasted_iota(jnp.int32, (ROWS, PAIR), 0)
    within = (
        lax.shift_right_logical(row, 5) * (2 * OUT_ROWS)
        + lax.bitwise_and(row, OUT_ROWS - 1)
        + (z * (2 * PAIR) + core * OUT_ROWS)
    )
    for i in range(NX):
        bank = lax.rem(x + (NX - i), NX) * (NZ * NYH * PAIR)
        ids[0, i * ROWS : (i + 1) * ROWS] = within + (bank + yh * PAIR)
        ids[1, i * ROWS : (i + 1) * ROWS] = within + (bank + (1 - yh) * PAIR)

    def names(s):
        return jnp.concatenate([labels[2 * s], labels[2 * s + 1]], axis=1)

    def first_pass(s, u):
        cosine = lax.dot_general(
            classes[u],
            feats[s],
            (((1,), (1,)), ((), ())),
            preferred_element_type=jnp.float32,
        )
        hit = ids[u] == names(s)
        logits = logit_scale * (cosine - jnp.where(hit, margin, 0.0))
        prob = jnp.exp(logits - logit_scale)
        probs[u, s] = prob
        total = jnp.sum(prob, axis=0, keepdims=True)
        target = jnp.sum(jnp.where(hit, logits, 0.0), axis=0, keepdims=True)
        sums[0, pl.ds(s, 1)] += total[:, :ROWS]
        sums[1, pl.ds(s, 1)] += total[:, ROWS:]
        targets[2 * s] += target[:, :ROWS]
        targets[2 * s + 1] += target[:, ROWS:]

    def receive_features(step):
        for h in range(2):
            feat_copies[step, h].wait_recv()
            if step < NZ // 2:
                feat_copies[step + 1, h].start()
            core_copies[step, h].start()
            if step < NZ // 2:
                back = NZ - step
                feat_copies[back, h].wait_recv()
                if step < NZ // 2 - 1:
                    feat_copies[back - 1, h].start()
                core_copies[back, h].start()
            if step == 2:
                class_copies[0, 1, h].wait_recv()
                for i in (2, 1, 3):
                    class_copies[i, 1, h].start()

    def receive_cores(*slots):
        for slot in slots:
            for h in range(2):
                core_copies[slot, h].wait_recv()

    def receive_classes(u):
        for i in range(1, NX):
            for h in range(2):
                class_copies[i, u, h].wait_recv()

    receive_features(1)
    receive_features(2)
    receive_classes(0)
    for one in label_copies:
        one.wait_recv()
    receive_cores(0, 1, 7)

    @pl.loop(0, 3)
    def _(k):
        first_pass(lax.rem(k + (NZ - 1), NZ), 0)

    receive_features(3)
    receive_cores(2, 6, 3, 5)

    @pl.loop(0, 4)
    def _(k):
        first_pass(2 + lax.div(k, 2) + lax.rem(k, 2) * (NZ - 4 - 2 * lax.div(k, 2)), 0)

    receive_features(4)
    receive_classes(1)
    receive_cores(4)

    @pl.loop(0, NZ + 1)
    def _(k):
        near = lax.div(NZ - k, NZ)
        first_pass(near * (NZ // 2) + (1 - near) * (k - 1), 1 - near)

    sum_copies, target_copies = {}, {}
    for o, w in plane:
        k = 2 * o + w
        sum_copies[o, w] = copy(
            sums, sums_in.at[k], sum_send.at[k], sum_recv.at[k], device(dz=o, dcore=w)
        )
        target_copies[o, w] = copy(
            targets.at[k],
            targets_in.at[k],
            target_send.at[k],
            target_recv.at[k],
            device(dz=NZ - o, dcore=w),
        )
    for one in sum_copies.values():
        one.start()
    for one in target_copies.values():
        one.start()
    whole = [sums[0], sums[1]]
    for (o, w), one in sum_copies.items():
        one.wait_recv()
        for q in range(2):
            other = sums_in[2 * o + w, (q + w) % 2]
            whole[q] += other if o == 0 else pltpu.roll(other, o, 0)
    for q in range(2):
        inverse_total[q] = 1.0 / whole[q]

    part_copies, north_copies = {}, {}
    for i in (2, 1, 3, 0):

        def weigh(s, carry):
            inverse = jnp.concatenate(
                [inverse_total[0, pl.ds(s, 1)], inverse_total[1, pl.ds(s, 1)]], axis=1
            )
            name = names(s)
            for u in range(2):
                rows = pl.ds(i * ROWS, ROWS)
                hit = jnp.where(ids[u, rows] == name, 1.0, 0.0)
                slope = probs[u, s, rows] * inverse - hit
                grads[s, u * ROWS : (u + 1) * ROWS] = slope.astype(jnp.bfloat16)
            return carry

        lax.fori_loop(0, NZ, weigh, 0)
        part = jnp.zeros((PAIR, WIDTH), jnp.float32)
        for s in range(NZ):
            part += jnp.dot(grads[s], feats[s], preferred_element_type=jnp.float32)
        north = part[:, EAST:].reshape(NYH * NYL, OUT_ROWS, NORTH)
        north_own[i] = north
        north_out[i] = north.astype(jnp.bfloat16)
        if i == 0:
            part_own[...] = part[:, :EAST]
        else:
            part_out[i] = part[:, :EAST].astype(jnp.bfloat16)
            part_copies[i] = copy(
                part_out.at[i],
                part_in.at[i],
                part_send.at[i],
                part_recv.at[i],
                device(dx=NX - i),
            )
            part_copies[i].start()
        for u, v in column:
            k = NYL * u + v
            north_copies[i, k] = copy(
                north_out.at[i, NYL * u + lax.rem(yl + v, NYL)],
                north_in.at[i, k],
                north_send.at[NX * k + i],
                north_recv.at[NX * k + i],
                device(dyh=u, dyl=v),
            )
            north_copies[i, k].start()

    own_target = targets[0]
    for (o, w), one in target_copies.items():
        one.wait_recv()
        own_target += targets_in[2 * o + w]
    loss_ref[...] = logit_scale + jnp.log(whole[0][0:1]) - own_target

    last_copies = {}
    for i in (2, 1, 3, 0):
        north = north_own[i, yl]
        for k in range(1, NYH * NYL):
            north_copies[i, k].wait_recv()
            north += north_in[i, k].astype(jnp.float32)
        if i > 0:
            last_out[i] = north.astype(jnp.bfloat16)
            last_copies[i] = copy(
                last_out.at[i],
                last_in.at[i],
                last_send.at[i],
                last_recv.at[i],
                device(dx=NX - i),
            )
            last_copies[i].start()

    half = part_own[...]
    for i in (1, 3, 2):
        part_copies[i].wait_recv()
        half += part_in[i].astype(jnp.float32)
    half = half.reshape(NYH * NYL, OUT_ROWS, EAST)
    half_own[...] = half
    half_out[...] = half.astype(jnp.bfloat16)
    half_copies = {}
    for u, v in column:
        k = NYL * u + v
        half_copies[u, v] = copy(
            half_out.at[NYL * u + lax.rem(yl + v, NYL)],
            half_in.at[k],
            half_send.at[k],
            half_recv.at[k],
            device(dyh=u, dyl=v),
        )
        half_copies[u, v].start()
    for i, one in last_copies.items():
        one.wait_recv()
        north += last_in[i].astype(jnp.float32)
    east = half_own[yl]
    for (u, v), one in half_copies.items():
        one.wait_recv()
        east += half_in[NYL * u + v].astype(jnp.float32)
    total = (logit_scale / 8.0) * jnp.concatenate([east, north], axis=1)
    unit = unit_ref[...]
    radial = jnp.sum(unit * total, axis=1, keepdims=True)
    grad_ref[...] = inverse_ref[...] * (total - unit * radial)

    for group in (
        feat_copies,
        core_copies,
        class_copies,
        sum_copies,
        target_copies,
        part_copies,
        half_copies,
        north_copies,
        last_copies,
    ):
        for one in group.values():
            one.wait_send()
    for one in label_copies:
        one.wait_send()


def head(unit_feats, labels, class_rows, unit_own, inverse_own):
    vmem = pl.BlockSpec(memory_space=pltpu.VMEM)
    dma = pltpu.SemaphoreType.DMA
    slots, column = NZ * NCORE, NYH * NYL
    scratch = [
        pltpu.VMEM((NZ, PAIR, WIDTH), jnp.bfloat16),
        pltpu.VMEM((2, BANKS, WIDTH), jnp.bfloat16),
        pltpu.VMEM((slots, 1, ROWS), jnp.int32),
        pltpu.VMEM((2, BANKS, PAIR), jnp.int32),
        pltpu.VMEM((2, NZ, BANKS, PAIR), jnp.float32),
        pltpu.VMEM((NZ, PAIR, PAIR), jnp.bfloat16),
        pltpu.VMEM((2, NZ, ROWS), jnp.float32),
        pltpu.VMEM((2, NZ, ROWS), jnp.float32),
        pltpu.VMEM((slots, 2, NZ, ROWS), jnp.float32),
        pltpu.VMEM((slots, 1, ROWS), jnp.float32),
        pltpu.VMEM((slots, 1, ROWS), jnp.float32),
        pltpu.VMEM((NX, PAIR, EAST), jnp.bfloat16),
        pltpu.VMEM((NX, PAIR, EAST), jnp.bfloat16),
        pltpu.VMEM((PAIR, EAST), jnp.float32),
        pltpu.VMEM((column, OUT_ROWS, EAST), jnp.bfloat16),
        pltpu.VMEM((column, OUT_ROWS, EAST), jnp.float32),
        pltpu.VMEM((column, OUT_ROWS, EAST), jnp.bfloat16),
        pltpu.VMEM((NX, column, OUT_ROWS, NORTH), jnp.bfloat16),
        pltpu.VMEM((NX, column, OUT_ROWS, NORTH), jnp.float32),
        pltpu.VMEM((NX, column, OUT_ROWS, NORTH), jnp.bfloat16),
        pltpu.VMEM((NX, OUT_ROWS, NORTH), jnp.bfloat16),
        pltpu.VMEM((NX, OUT_ROWS, NORTH), jnp.bfloat16),
    ]
    counts = (2 * NZ, 2 * NZ, slots, 4 * NX, slots, slots, NX, column, NX * column, NX)
    for count in counts:
        scratch += [dma((count,)), dma((count,))]
    return pl.pallas_call(
        head_kernel,
        out_shape=(
            jax.ShapeDtypeStruct((1, ROWS), jnp.float32),
            jax.ShapeDtypeStruct((OUT_ROWS, WIDTH), jnp.float32),
        ),
        in_specs=[vmem] * 5,
        out_specs=(vmem, vmem),
        scratch_shapes=scratch,
        compiler_params=pltpu.CompilerParams(
            collective_id=0, has_side_effects=True, vmem_limit_bytes=48 * 1024 * 1024
        ),
    )(unit_feats, labels, class_rows, unit_own, inverse_own)


def per_device(features, labels, weights, sampled):
    dp = lax.axis_index("dp")
    core, yl = dp % NCORE, dp // NCORE
    feat_wide = features.astype(jnp.float32)
    unit_feats = (feat_wide * normalize_rows(feat_wide)).astype(jnp.bfloat16)
    picked = lax.dynamic_index_in_dim(
        sampled.reshape(NYL, NCORE, OUT_ROWS), core, axis=1, keepdims=False
    ).reshape(ROWS)
    chosen = weights[picked]
    inverse_norm = normalize_rows(chosen)
    unit_f32 = chosen * inverse_norm
    unit_own = lax.dynamic_slice_in_dim(unit_f32, yl * OUT_ROWS, OUT_ROWS)
    inverse_own = lax.dynamic_slice_in_dim(inverse_norm, yl * OUT_ROWS, OUT_ROWS)
    loss, grad = head(
        unit_feats,
        labels.reshape(1, ROWS),
        unit_f32.astype(jnp.bfloat16),
        unit_own,
        inverse_own,
    )
    return (loss.reshape(ROWS), grad)


def solution(mesh):
    in_specs = (P(("cls", "dp"), None), P(("cls", "dp")), P("cls", None), P("cls"))
    out_specs = (P(("cls", "dp")), P(("cls", "dp"), None))
    return jax.shard_map(
        per_device, mesh=mesh, in_specs=in_specs, out_specs=out_specs, check_vma=False
    )
```

```python
import functools

import jax
import jax.numpy as jnp
from jax import lax
from jax.experimental import pallas as pl
from jax.experimental.pallas import tpu as pltpu
from jax.sharding import PartitionSpec as P

logit_scale = 64.0
margin = 0.35
epsilon = 1e-06

NX, NZ, NYH, NYL, NCORE = 4, 8, 2, 4, 2
ROWS = 128
OUT_ROWS = 32
BANK = 1024
WIDTH = 512
PAIR = 2 * ROWS
HALF = ROWS // 2
QUARTER = ROWS // 4
BANKS = NX * ROWS
EAST = 384
NORTH = WIDTH - EAST


def normalize_rows(matrix):
    squares = jnp.sum(matrix * matrix, axis=1, keepdims=True)
    return lax.rsqrt(squares + epsilon)


def head_kernel(
    feat_ref,
    label_ref,
    bank_ref,
    sampled_ref,
    loss_ref,
    grad_ref,
    feats,
    classes,
    labels,
    ids,
    probs,
    grads,
    inverse_total,
    sums,
    sums_in,
    targets,
    targets_in,
    part_out,
    part_in,
    part_own,
    half_out,
    half_own,
    half_in,
    north_out,
    north_own,
    north_in,
    last_out,
    last_in,
    feat_in,
    places,
    bank,
    chosen,
    load_sem,
    feat_send,
    feat_recv,
    core_send,
    core_recv,
    label_send,
    label_recv,
    class_send,
    class_recv,
    sum_send,
    sum_recv,
    target_send,
    target_recv,
    part_send,
    part_recv,
    half_send,
    half_recv,
    north_send,
    north_recv,
    last_send,
    last_recv,
):
    cls, dp = lax.axis_index("cls"), lax.axis_index("dp")
    x, z, yh = lax.div(cls, 16), lax.rem(lax.div(cls, 2), 8), lax.rem(cls, 2)
    yl, core = lax.div(dp, 2), lax.rem(dp, 2)

    def device(dx=0, dz=0, dyh=0, dyl=0, dcore=0):
        px = lax.rem(x + dx, NX)
        pz = lax.rem(z + dz, NZ)
        pyh = lax.rem(yh + dyh, NYH)
        pyl = lax.rem(yl + dyl, NYL)
        pcore = lax.rem(core + dcore, NCORE)
        return ((px * NZ + pz) * NYH + pyh, pyl * NCORE + pcore)

    mirror = ((x * NZ + z) * NYH + (1 - yh), (NYL - 1 - yl) * NCORE + core)

    def copy(src, dst, send, recv, target):
        return pltpu.make_async_remote_copy(
            src_ref=src,
            dst_ref=dst,
            send_sem=send,
            recv_sem=recv,
            device_id=target,
            device_id_type=pl.DeviceIdType.MESH,
        )

    plane = [(o, w) for o in range(NZ) for w in range(NCORE) if (o, w) != (0, 0)]
    column = [(u, v) for u in range(NYH) for v in range(NYL) if (u, v) != (0, 0)]

    feat_load = pltpu.make_async_copy(feat_ref, feat_in, load_sem.at[0])
    label_load = pltpu.make_async_copy(label_ref, labels.at[0], load_sem.at[1])
    sampled_load = pltpu.make_async_copy(sampled_ref, places, load_sem.at[2])
    bank_load = pltpu.make_async_copy(bank_ref, bank, load_sem.at[3])
    for one in (feat_load, label_load, sampled_load, bank_load):
        one.start()
    barrier = pltpu.get_barrier_semaphore()
    peers = [device(dz=o, dcore=w) for o, w in plane]
    peers += [device(dx=i) for i in range(1, NX)]
    peers += [device(dyh=u, dyl=v) for u, v in column]
    for peer in peers:
        pl.semaphore_signal(barrier, inc=1, device_id=peer, device_id_type=pl.DeviceIdType.MESH)
    feat_load.wait()
    feat_wide = feat_in[...].astype(jnp.float32)
    feats[0, :ROWS] = (feat_wide * normalize_rows(feat_wide)).astype(jnp.bfloat16)
    label_load.wait()
    sums[...] = jnp.zeros_like(sums)
    targets[...] = jnp.zeros_like(targets)
    pl.semaphore_wait(barrier, len(peers))

    def feat_copy(slot, h):
        if slot < NZ // 2 or (slot == NZ // 2 and h < 2):
            came, target = slot - 1, device(dz=1)
        else:
            came, target = (slot + 1) % NZ, device(dz=NZ - 1)
        rows = pl.ds(h * QUARTER, QUARTER)
        k = 4 * slot + h
        return copy(
            feats.at[came, rows], feats.at[slot, rows], feat_send.at[k], feat_recv.at[k], target
        )

    def core_copy(slot, h):
        rows = pl.ds(h * HALF, HALF)
        k = 2 * slot + h
        return copy(
            feats.at[slot, rows],
            feats.at[slot, pl.ds(ROWS + h * HALF, HALF)],
            core_send.at[k],
            core_recv.at[k],
            device(dcore=1),
        )

    def class_copy(i, u, h):
        rows = pl.ds(i * ROWS + h * HALF, HALF)
        near = pl.ds(h * HALF, HALF)
        if i == 0:
            target = mirror
        else:
            target = device(dx=i)
        k = 4 * i + 2 * u + h
        src = classes.at[1 if i and u else 0, near]
        return copy(src, classes.at[u, rows], class_send.at[k], class_recv.at[k], target)

    def label_copy(o, w):
        k = 2 * o + w
        return copy(
            labels.at[0], labels.at[k], label_send.at[k], label_recv.at[k], device(dz=o, dcore=w)
        )

    feat_copies = {(s, h): feat_copy(s, h) for s in range(1, NZ) for h in range(4)}
    core_copies = {(s, h): core_copy(s, h) for s in range(NZ) for h in range(2)}
    class_copies = {
        (i, u, h): class_copy(i, u, h)
        for i in range(NX)
        for u in range(2)
        for h in range(2)
        if i + u
    }
    label_copies = [label_copy(o, w) for o, w in plane]

    for h in range(4):
        feat_copies[1, h].start()
        feat_copies[NZ - 1, h].start()
    for h in range(2):
        core_copies[0, h].start()
    for one in label_copies:
        one.start()

    sampled_load.wait()
    bank_load.wait()

    @pl.loop(0, ROWS // 8)
    def _(block):
        for r in range(8):
            k = block * 8 + r
            place = lax.div(k, OUT_ROWS) * (2 * OUT_ROWS) + core * OUT_ROWS + lax.rem(k, OUT_ROWS)
            chosen[pl.ds(k, 1)] = bank[pl.ds(places[place], 1)]

    picked = chosen[...]
    classes[0, :ROWS] = (picked * normalize_rows(picked)).astype(jnp.bfloat16)
    row = lax.broadcasted_iota(jnp.int32, (ROWS, PAIR), 0)
    within = (
        lax.shift_right_logical(row, 5) * (2 * OUT_ROWS)
        + lax.bitwise_and(row, OUT_ROWS - 1)
        + (z * (2 * PAIR) + core * OUT_ROWS)
    )
    for i in range(NX):
        base = lax.rem(x + (NX - i), NX) * (NZ * NYH * PAIR)
        ids[0, i * ROWS : (i + 1) * ROWS] = within + (base + yh * PAIR)
        ids[1, i * ROWS : (i + 1) * ROWS] = within + (base + (1 - yh) * PAIR)
    for h in range(2):
        class_copies[0, 1, h].start()
    for i in (2, 1, 3):
        for h in range(2):
            class_copies[i, 0, h].start()

    def names(s):
        return jnp.concatenate([labels[2 * s], labels[2 * s + 1]], axis=1)

    def first_pass(s, u):
        cosine = lax.dot_general(
            classes[u],
            feats[s],
            (((1,), (1,)), ((), ())),
            preferred_element_type=jnp.float32,
        )
        hit = ids[u] == names(s)
        logits = logit_scale * (cosine - jnp.where(hit, margin, 0.0))
        prob = jnp.exp(logits - logit_scale)
        probs[u, s] = prob
        total = jnp.sum(prob, axis=0, keepdims=True)
        target = jnp.sum(jnp.where(hit, logits, 0.0), axis=0, keepdims=True)
        sums[0, pl.ds(s, 1)] += total[:, :ROWS]
        sums[1, pl.ds(s, 1)] += total[:, ROWS:]
        targets[2 * s] += target[:, :ROWS]
        targets[2 * s + 1] += target[:, ROWS:]

    def receive_features(step):
        back = NZ - step
        for h in range(4):
            if step < NZ // 2:
                feat_copies[step, h].wait_recv()
                if step + 1 < NZ // 2 or h < 2:
                    feat_copies[step + 1, h].start()
                feat_copies[back, h].wait_recv()
                if step + 1 < NZ // 2 or h >= 2:
                    feat_copies[back - 1, h].start()
                if h % 2:
                    core_copies[step, h // 2].start()
                    core_copies[back, h // 2].start()
            if step == 2 and h % 2:
                class_copies[0, 1, h // 2].wait_recv()
                for i in (2, 1, 3):
                    class_copies[i, 1, h // 2].start()
        if step == NZ // 2:
            for h in (0, 2, 1, 3):
                feat_copies[step, h].wait_recv()
                if h in (1, 3):
                    core_copies[step, h // 2].start()

    def receive_cores(*slots):
        for slot in slots:
            for h in range(2):
                core_copies[slot, h].wait_recv()

    def receive_classes(u):
        for i in range(1, NX):
            for h in range(2):
                class_copies[i, u, h].wait_recv()

    receive_features(1)
    receive_features(2)
    receive_classes(0)
    for one in label_copies:
        one.wait_recv()
    receive_cores(0, 1, 7)

    @pl.loop(0, 3)
    def _(k):
        first_pass(lax.rem(k + (NZ - 1), NZ), 0)

    receive_features(3)
    receive_cores(2, 6, 3, 5)

    @pl.loop(0, 4)
    def _(k):
        first_pass(2 + lax.div(k, 2) + lax.rem(k, 2) * (NZ - 4 - 2 * lax.div(k, 2)), 0)

    receive_classes(1)

    @pl.loop(0, 3)
    def _(k):
        first_pass(lax.rem(k + (NZ - 1), NZ), 1)

    receive_features(4)

    @pl.loop(0, 4)
    def _(k):
        first_pass(2 + lax.div(k, 2) + lax.rem(k, 2) * (NZ - 4 - 2 * lax.div(k, 2)), 1)

    receive_cores(4)

    @pl.loop(0, 2)
    def _(k):
        first_pass(NZ // 2, k)

    sum_copies, target_copies = {}, {}
    for o, w in plane:
        k = 2 * o + w
        sum_copies[o, w] = copy(
            sums, sums_in.at[k], sum_send.at[k], sum_recv.at[k], device(dz=o, dcore=w)
        )
        target_copies[o, w] = copy(
            targets.at[k],
            targets_in.at[k],
            target_send.at[k],
            target_recv.at[k],
            device(dz=NZ - o, dcore=w),
        )
    for one in sum_copies.values():
        one.start()
    for one in target_copies.values():
        one.start()
    whole = [sums[0], sums[1]]
    for (o, w), one in sum_copies.items():
        one.wait_recv()
        for q in range(2):
            other = sums_in[2 * o + w, (q + w) % 2]
            whole[q] += other if o == 0 else pltpu.roll(other, o, 0)
    for q in range(2):
        inverse_total[q] = 1.0 / whole[q]

    part_copies, north_copies = {}, {}
    for i in (2, 1, 3, 0):

        def weigh(s, carry):
            inverse = jnp.concatenate(
                [inverse_total[0, pl.ds(s, 1)], inverse_total[1, pl.ds(s, 1)]], axis=1
            )
            name = names(s)
            for u in range(2):
                rows = pl.ds(i * ROWS, ROWS)
                hit = jnp.where(ids[u, rows] == name, 1.0, 0.0)
                slope = probs[u, s, rows] * inverse - hit
                grads[s, u * ROWS : (u + 1) * ROWS] = slope.astype(jnp.bfloat16)
            return carry

        lax.fori_loop(0, NZ, weigh, 0)
        part = jnp.zeros((PAIR, WIDTH), jnp.float32)
        for s in range(NZ):
            part += jnp.dot(grads[s], feats[s], preferred_element_type=jnp.float32)
        north = part[:, EAST:].reshape(NYH * NYL, OUT_ROWS, NORTH)
        north_own[i] = north
        north_out[i] = north.astype(jnp.bfloat16)
        if i == 0:
            part_own[...] = part[:, :EAST]
        else:
            part_out[i] = part[:, :EAST].astype(jnp.bfloat16)
            part_copies[i] = copy(
                part_out.at[i],
                part_in.at[i],
                part_send.at[i],
                part_recv.at[i],
                device(dx=NX - i),
            )
            part_copies[i].start()
        for u, v in column:
            k = NYL * u + v
            north_copies[i, k] = copy(
                north_out.at[i, NYL * u + lax.rem(yl + v, NYL)],
                north_in.at[i, k],
                north_send.at[NX * k + i],
                north_recv.at[NX * k + i],
                device(dyh=u, dyl=v),
            )
            north_copies[i, k].start()

    own_target = targets[0]
    for (o, w), one in target_copies.items():
        one.wait_recv()
        own_target += targets_in[2 * o + w]
    loss_ref[...] = logit_scale + jnp.log(whole[0][0:1]) - own_target

    last_copies = {}
    for i in (2, 1, 3, 0):
        north = north_own[i, yl]
        for k in range(1, NYH * NYL):
            north_copies[i, k].wait_recv()
            north += north_in[i, k].astype(jnp.float32)
        if i > 0:
            last_out[i] = north.astype(jnp.bfloat16)
            last_copies[i] = copy(
                last_out.at[i],
                last_in.at[i],
                last_send.at[i],
                last_recv.at[i],
                device(dx=NX - i),
            )
            last_copies[i].start()

    half = part_own[...]
    for i in (1, 3, 2):
        part_copies[i].wait_recv()
        half += part_in[i].astype(jnp.float32)
    half = half.reshape(NYH * NYL, OUT_ROWS, EAST)
    half_own[...] = half
    half_out[...] = half.astype(jnp.bfloat16)
    half_copies = {}
    for u, v in column:
        k = NYL * u + v
        half_copies[u, v] = copy(
            half_out.at[NYL * u + lax.rem(yl + v, NYL)],
            half_in.at[k],
            half_send.at[k],
            half_recv.at[k],
            device(dyh=u, dyl=v),
        )
        half_copies[u, v].start()
    for i, one in last_copies.items():
        one.wait_recv()
        north += last_in[i].astype(jnp.float32)
    east = half_own[yl]
    for (u, v), one in half_copies.items():
        one.wait_recv()
        east += half_in[NYL * u + v].astype(jnp.float32)
    total = (logit_scale / 8.0) * jnp.concatenate([east, north], axis=1)
    own = chosen[pl.ds(pl.multiple_of(yl * OUT_ROWS, OUT_ROWS), OUT_ROWS)]
    inverse = normalize_rows(own)
    unit = own * inverse
    radial = jnp.sum(unit * total, axis=1, keepdims=True)
    grad_ref[...] = inverse * (total - unit * radial)

    for group in (
        feat_copies,
        core_copies,
        class_copies,
        sum_copies,
        target_copies,
        part_copies,
        half_copies,
        north_copies,
        last_copies,
    ):
        for one in group.values():
            one.wait_send()
    for one in label_copies:
        one.wait_send()


def head(features, labels, weights, sampled):
    vmem = pl.BlockSpec(memory_space=pltpu.VMEM)
    dma = pltpu.SemaphoreType.DMA
    slots, column = NZ * NCORE, NYH * NYL
    scratch = [
        pltpu.VMEM((NZ, PAIR, WIDTH), jnp.bfloat16),
        pltpu.VMEM((2, BANKS, WIDTH), jnp.bfloat16),
        pltpu.VMEM((slots, 1, ROWS), jnp.int32),
        pltpu.VMEM((2, BANKS, PAIR), jnp.int32),
        pltpu.VMEM((2, NZ, BANKS, PAIR), jnp.float32),
        pltpu.VMEM((NZ, PAIR, PAIR), jnp.bfloat16),
        pltpu.VMEM((2, NZ, ROWS), jnp.float32),
        pltpu.VMEM((2, NZ, ROWS), jnp.float32),
        pltpu.VMEM((slots, 2, NZ, ROWS), jnp.float32),
        pltpu.VMEM((slots, 1, ROWS), jnp.float32),
        pltpu.VMEM((slots, 1, ROWS), jnp.float32),
        pltpu.VMEM((NX, PAIR, EAST), jnp.bfloat16),
        pltpu.VMEM((NX, PAIR, EAST), jnp.bfloat16),
        pltpu.VMEM((PAIR, EAST), jnp.float32),
        pltpu.VMEM((column, OUT_ROWS, EAST), jnp.bfloat16),
        pltpu.VMEM((column, OUT_ROWS, EAST), jnp.float32),
        pltpu.VMEM((column, OUT_ROWS, EAST), jnp.bfloat16),
        pltpu.VMEM((NX, column, OUT_ROWS, NORTH), jnp.bfloat16),
        pltpu.VMEM((NX, column, OUT_ROWS, NORTH), jnp.float32),
        pltpu.VMEM((NX, column, OUT_ROWS, NORTH), jnp.bfloat16),
        pltpu.VMEM((NX, OUT_ROWS, NORTH), jnp.bfloat16),
        pltpu.VMEM((NX, OUT_ROWS, NORTH), jnp.bfloat16),
        pltpu.VMEM((ROWS, WIDTH), jnp.bfloat16),
        pltpu.SMEM((PAIR,), jnp.int32),
        pltpu.VMEM((BANK, WIDTH), jnp.float32),
        pltpu.VMEM((ROWS, WIDTH), jnp.float32),
        dma((4,)),
    ]
    counts = (4 * NZ, 2 * NZ, slots, 4 * NX, slots, slots, NX, column, NX * column, NX)
    for count in counts:
        scratch += [dma((count,)), dma((count,))]
    return pl.pallas_call(
        head_kernel,
        out_shape=(
            jax.ShapeDtypeStruct((1, ROWS), jnp.float32),
            jax.ShapeDtypeStruct((OUT_ROWS, WIDTH), jnp.float32),
        ),
        in_specs=[pl.BlockSpec(memory_space=pl.ANY)] * 4,
        out_specs=(vmem, vmem),
        scratch_shapes=scratch,
        compiler_params=pltpu.CompilerParams(collective_id=0, has_side_effects=True),
    )(features, labels, weights, sampled)


def per_device(features, labels, weights, sampled):
    loss, grad = head(features, labels.reshape(1, ROWS), weights, sampled)
    return (loss.reshape(ROWS), grad)


def solution(mesh):
    in_specs = (P(("cls", "dp"), None), P(("cls", "dp")), P("cls", None), P("cls"))
    out_specs = (P(("cls", "dp")), P(("cls", "dp"), None))
    return jax.shard_map(
        per_device, mesh=mesh, in_specs=in_specs, out_specs=out_specs, check_vma=False
    )
```

```python
import functools

import jax
import jax.numpy as jnp
from jax import lax
from jax.experimental import pallas as pl
from jax.experimental.pallas import tpu as pltpu
from jax.sharding import PartitionSpec as P

logit_scale = 64.0
margin = 0.35
epsilon = 1e-06

NX, NZ, NYH, NYL, NCORE = 4, 8, 2, 4, 2
ROWS = 128
OUT_ROWS = 32
BANK = 1024
WIDTH = 512
PAIR = 2 * ROWS
HALF = ROWS // 2
QUARTER = ROWS // 4
BANKS = NX * ROWS
EAST = 384
NORTH = WIDTH - EAST
EAST_CUTS = ((0, 256), (256, 128))


def normalize_rows(matrix):
    squares = jnp.sum(matrix * matrix, axis=1, keepdims=True)
    return lax.rsqrt(squares + epsilon)


def head_kernel(
    feat_ref,
    label_ref,
    bank_ref,
    sampled_ref,
    loss_ref,
    grad_ref,
    feats,
    classes,
    labels,
    ids,
    probs,
    grads,
    inverse_total,
    sums,
    sums_in,
    targets,
    targets_in,
    part_out,
    part_in,
    part_own,
    half_out,
    half_own,
    half_in,
    north_out,
    north_own,
    north_in,
    last_out,
    last_in,
    feat_in,
    places,
    bank,
    chosen,
    load_sem,
    feat_send,
    feat_recv,
    core_send,
    core_recv,
    label_send,
    label_recv,
    class_send,
    class_recv,
    sum_send,
    sum_recv,
    target_send,
    target_recv,
    part_send,
    part_recv,
    half_send,
    half_recv,
    north_send,
    north_recv,
    last_send,
    last_recv,
):
    cls, dp = lax.axis_index("cls"), lax.axis_index("dp")
    x, z, yh = lax.div(cls, 16), lax.rem(lax.div(cls, 2), 8), lax.rem(cls, 2)
    yl, core = lax.div(dp, 2), lax.rem(dp, 2)

    def device(dx=0, dz=0, dyh=0, dyl=0, dcore=0):
        px = lax.rem(x + dx, NX)
        pz = lax.rem(z + dz, NZ)
        pyh = lax.rem(yh + dyh, NYH)
        pyl = lax.rem(yl + dyl, NYL)
        pcore = lax.rem(core + dcore, NCORE)
        return ((px * NZ + pz) * NYH + pyh, pyl * NCORE + pcore)

    mirror = ((x * NZ + z) * NYH + (1 - yh), (NYL - 1 - yl) * NCORE + core)

    def copy(src, dst, send, recv, target):
        return pltpu.make_async_remote_copy(
            src_ref=src,
            dst_ref=dst,
            send_sem=send,
            recv_sem=recv,
            device_id=target,
            device_id_type=pl.DeviceIdType.MESH,
        )

    plane = [(o, w) for o in range(NZ) for w in range(NCORE) if (o, w) != (0, 0)]
    column = [(u, v) for u in range(NYH) for v in range(NYL) if (u, v) != (0, 0)]

    feat_load = pltpu.make_async_copy(feat_ref, feat_in, load_sem.at[0])
    label_load = pltpu.make_async_copy(label_ref, labels.at[0], load_sem.at[1])
    sampled_load = pltpu.make_async_copy(sampled_ref, places, load_sem.at[2])
    bank_load = pltpu.make_async_copy(bank_ref, bank, load_sem.at[3])
    for one in (feat_load, label_load, sampled_load, bank_load):
        one.start()
    barrier = pltpu.get_barrier_semaphore()
    peers = [device(dz=o, dcore=w) for o, w in plane]
    peers += [device(dx=i) for i in range(1, NX)]
    peers += [device(dyh=u, dyl=v) for u, v in column]
    for peer in peers:
        pl.semaphore_signal(barrier, inc=1, device_id=peer, device_id_type=pl.DeviceIdType.MESH)
    feat_load.wait()
    feat_wide = feat_in[...].astype(jnp.float32)
    feats[0, :ROWS] = (feat_wide * normalize_rows(feat_wide)).astype(jnp.bfloat16)
    label_load.wait()
    sums[...] = jnp.zeros_like(sums)
    targets[...] = jnp.zeros_like(targets)
    pl.semaphore_wait(barrier, len(peers))

    def feat_copy(slot, h):
        if slot < NZ // 2 or (slot == NZ // 2 and h < 2):
            came, target = slot - 1, device(dz=1)
        else:
            came, target = (slot + 1) % NZ, device(dz=NZ - 1)
        rows = pl.ds(h * QUARTER, QUARTER)
        k = 4 * slot + h
        return copy(
            feats.at[came, rows], feats.at[slot, rows], feat_send.at[k], feat_recv.at[k], target
        )

    def core_copy(slot, h):
        rows = pl.ds(h * HALF, HALF)
        k = 2 * slot + h
        return copy(
            feats.at[slot, rows],
            feats.at[slot, pl.ds(ROWS + h * HALF, HALF)],
            core_send.at[k],
            core_recv.at[k],
            device(dcore=1),
        )

    def class_copy(i, u, h):
        rows = pl.ds(i * ROWS + h * HALF, HALF)
        near = pl.ds(h * HALF, HALF)
        if i == 0:
            target = mirror
        else:
            target = device(dx=i)
        k = 4 * i + 2 * u + h
        src = classes.at[1 if i and u else 0, near]
        return copy(src, classes.at[u, rows], class_send.at[k], class_recv.at[k], target)

    def label_copy(o, w):
        k = 2 * o + w
        return copy(
            labels.at[0], labels.at[k], label_send.at[k], label_recv.at[k], device(dz=o, dcore=w)
        )

    feat_copies = {(s, h): feat_copy(s, h) for s in range(1, NZ) for h in range(4)}
    core_copies = {(s, h): core_copy(s, h) for s in range(NZ) for h in range(2)}
    class_copies = {
        (i, u, h): class_copy(i, u, h)
        for i in range(NX)
        for u in range(2)
        for h in range(2)
        if i + u
    }
    label_copies = [label_copy(o, w) for o, w in plane]

    for h in range(4):
        feat_copies[1, h].start()
        feat_copies[NZ - 1, h].start()
    for h in range(2):
        core_copies[0, h].start()
    for one in label_copies:
        one.start()

    sampled_load.wait()
    bank_load.wait()

    @pl.loop(0, ROWS // 8)
    def _(block):
        for r in range(8):
            k = block * 8 + r
            place = lax.div(k, OUT_ROWS) * (2 * OUT_ROWS) + core * OUT_ROWS + lax.rem(k, OUT_ROWS)
            chosen[pl.ds(k, 1)] = bank[pl.ds(places[place], 1)]

    picked = chosen[...]
    classes[0, :ROWS] = (picked * normalize_rows(picked)).astype(jnp.bfloat16)
    row = lax.broadcasted_iota(jnp.int32, (ROWS, PAIR), 0)
    within = (
        lax.shift_right_logical(row, 5) * (2 * OUT_ROWS)
        + lax.bitwise_and(row, OUT_ROWS - 1)
        + (z * (2 * PAIR) + core * OUT_ROWS)
    )
    for i in range(NX):
        base = lax.rem(x + (NX - i), NX) * (NZ * NYH * PAIR)
        ids[0, i * ROWS : (i + 1) * ROWS] = within + (base + yh * PAIR)
        ids[1, i * ROWS : (i + 1) * ROWS] = within + (base + (1 - yh) * PAIR)
    for h in range(2):
        class_copies[0, 1, h].start()
    for i in (2, 1, 3):
        for h in range(2):
            class_copies[i, 0, h].start()

    def names(s):
        return jnp.concatenate([labels[2 * s], labels[2 * s + 1]], axis=1)

    def first_pass(s, u):
        cosine = lax.dot_general(
            classes[u],
            feats[s],
            (((1,), (1,)), ((), ())),
            preferred_element_type=jnp.float32,
        )
        hit = ids[u] == names(s)
        logits = logit_scale * (cosine - jnp.where(hit, margin, 0.0))
        prob = jnp.exp(logits - logit_scale)
        probs[u, s] = prob
        total = jnp.sum(prob, axis=0, keepdims=True)
        target = jnp.sum(jnp.where(hit, logits, 0.0), axis=0, keepdims=True)
        sums[0, pl.ds(s, 1)] += total[:, :ROWS]
        sums[1, pl.ds(s, 1)] += total[:, ROWS:]
        targets[2 * s] += target[:, :ROWS]
        targets[2 * s + 1] += target[:, ROWS:]

    def receive_features(step):
        back = NZ - step
        for h in range(4):
            if step < NZ // 2:
                feat_copies[step, h].wait_recv()
                if step + 1 < NZ // 2 or h < 2:
                    feat_copies[step + 1, h].start()
                feat_copies[back, h].wait_recv()
                if step + 1 < NZ // 2 or h >= 2:
                    feat_copies[back - 1, h].start()
                if h % 2:
                    core_copies[step, h // 2].start()
                    core_copies[back, h // 2].start()
            if step == 2 and h % 2:
                class_copies[0, 1, h // 2].wait_recv()
                for i in (2, 1, 3):
                    class_copies[i, 1, h // 2].start()
        if step == NZ // 2:
            for h in (0, 2, 1, 3):
                feat_copies[step, h].wait_recv()
                if h in (1, 3):
                    core_copies[step, h // 2].start()

    def receive_cores(*slots):
        for slot in slots:
            for h in range(2):
                core_copies[slot, h].wait_recv()

    def receive_classes(u):
        for i in range(1, NX):
            for h in range(2):
                class_copies[i, u, h].wait_recv()

    receive_features(1)
    receive_features(2)
    receive_classes(0)
    for one in label_copies:
        one.wait_recv()
    receive_cores(0, 1, 7)

    @pl.loop(0, 3)
    def _(k):
        first_pass(lax.rem(k + (NZ - 1), NZ), 0)

    receive_features(3)
    receive_cores(2, 6, 3, 5)

    @pl.loop(0, 4)
    def _(k):
        first_pass(2 + lax.div(k, 2) + lax.rem(k, 2) * (NZ - 4 - 2 * lax.div(k, 2)), 0)

    receive_classes(1)

    @pl.loop(0, 3)
    def _(k):
        first_pass(lax.rem(k + (NZ - 1), NZ), 1)

    receive_features(4)

    @pl.loop(0, 4)
    def _(k):
        first_pass(2 + lax.div(k, 2) + lax.rem(k, 2) * (NZ - 4 - 2 * lax.div(k, 2)), 1)

    receive_cores(4)

    @pl.loop(0, 2)
    def _(k):
        first_pass(NZ // 2, k)

    sum_copies, target_copies = {}, {}
    for o, w in plane:
        k = 2 * o + w
        sum_copies[o, w] = copy(
            sums, sums_in.at[k], sum_send.at[k], sum_recv.at[k], device(dz=o, dcore=w)
        )
        target_copies[o, w] = copy(
            targets.at[k],
            targets_in.at[k],
            target_send.at[k],
            target_recv.at[k],
            device(dz=NZ - o, dcore=w),
        )
    for one in sum_copies.values():
        one.start()
    for one in target_copies.values():
        one.start()
    whole = [sums[0], sums[1]]
    for (o, w), one in sum_copies.items():
        one.wait_recv()
        for q in range(2):
            other = sums_in[2 * o + w, (q + w) % 2]
            whole[q] += other if o == 0 else pltpu.roll(other, o, 0)
    for q in range(2):
        inverse_total[q] = 1.0 / whole[q]

    part_copies, north_copies = {}, {}

    def send_part(turn, i):
        columns = pl.ds(*EAST_CUTS[turn])
        part_copies[turn, i] = copy(
            part_out.at[i, :, columns],
            part_in.at[i, :, columns],
            part_send.at[NX * turn + i],
            part_recv.at[NX * turn + i],
            device(dx=NX - i),
        )
        part_copies[turn, i].start()

    for i in (2, 1, 3, 0):

        def weigh(s, carry):
            inverse = jnp.concatenate(
                [inverse_total[0, pl.ds(s, 1)], inverse_total[1, pl.ds(s, 1)]], axis=1
            )
            name = names(s)
            for u in range(2):
                rows = pl.ds(i * ROWS, ROWS)
                hit = jnp.where(ids[u, rows] == name, 1.0, 0.0)
                slope = probs[u, s, rows] * inverse - hit
                grads[s, u * ROWS : (u + 1) * ROWS] = slope.astype(jnp.bfloat16)
            return carry

        lax.fori_loop(0, NZ, weigh, 0)
        part = jnp.zeros((PAIR, WIDTH), jnp.float32)
        for s in range(NZ):
            part += jnp.dot(grads[s], feats[s], preferred_element_type=jnp.float32)
        north = part[:, EAST:].reshape(NYH * NYL, OUT_ROWS, NORTH)
        north_own[i] = north
        north_out[i] = north.astype(jnp.bfloat16)
        if i == 0:
            part_own[...] = part[:, :EAST]
        else:
            part_out[i] = part[:, :EAST].astype(jnp.bfloat16)
            send_part(0, i)
        for u, v in column:
            k = NYL * u + v
            north_copies[i, k] = copy(
                north_out.at[i, NYL * u + lax.rem(yl + v, NYL)],
                north_in.at[i, k],
                north_send.at[NX * k + i],
                north_recv.at[NX * k + i],
                device(dyh=u, dyl=v),
            )
            north_copies[i, k].start()

    for i in (2, 1, 3):
        send_part(1, i)

    own_target = targets[0]
    for (o, w), one in target_copies.items():
        one.wait_recv()
        own_target += targets_in[2 * o + w]
    loss_ref[...] = logit_scale + jnp.log(whole[0][0:1]) - own_target

    last_copies = {}
    for i in (2, 1, 3, 0):
        north = north_own[i, yl]
        for k in range(1, NYH * NYL):
            north_copies[i, k].wait_recv()
            north += north_in[i, k].astype(jnp.float32)
        if i > 0:
            last_out[i] = north.astype(jnp.bfloat16)
            last_copies[i] = copy(
                last_out.at[i],
                last_in.at[i],
                last_send.at[i],
                last_recv.at[i],
                device(dx=NX - i),
            )
            last_copies[i].start()

    half_copies = {}
    for turn, (start, width) in enumerate(EAST_CUTS):
        columns = slice(start, start + width)
        half = part_own[:, columns]
        for i in (1, 3, 2):
            part_copies[turn, i].wait_recv()
            half += part_in[i, :, columns].astype(jnp.float32)
        half = half.reshape(NYH * NYL, OUT_ROWS, width)
        half_own[:, :, columns] = half
        half_out[:, :, columns] = half.astype(jnp.bfloat16)
        for u, v in column:
            k = NYL * u + v
            half_copies[turn, k] = copy(
                half_out.at[NYL * u + lax.rem(yl + v, NYL), :, pl.ds(start, width)],
                half_in.at[k, :, pl.ds(start, width)],
                half_send.at[NYH * NYL * turn + k],
                half_recv.at[NYH * NYL * turn + k],
                device(dyh=u, dyl=v),
            )
            half_copies[turn, k].start()
    for i, one in last_copies.items():
        one.wait_recv()
        north += last_in[i].astype(jnp.float32)
    pieces = []
    for turn, (start, width) in enumerate(EAST_CUTS):
        columns = slice(start, start + width)
        piece = half_own[yl, :, columns]
        for k in range(1, NYH * NYL):
            half_copies[turn, k].wait_recv()
            piece += half_in[k, :, columns].astype(jnp.float32)
        pieces.append(piece)
    pieces.append(north)
    total = (logit_scale / 8.0) * jnp.concatenate(pieces, axis=1)
    own = chosen[pl.ds(pl.multiple_of(yl * OUT_ROWS, OUT_ROWS), OUT_ROWS)]
    inverse = normalize_rows(own)
    unit = own * inverse
    radial = jnp.sum(unit * total, axis=1, keepdims=True)
    grad_ref[...] = inverse * (total - unit * radial)

    for group in (
        feat_copies,
        core_copies,
        class_copies,
        sum_copies,
        target_copies,
        part_copies,
        half_copies,
        north_copies,
        last_copies,
    ):
        for one in group.values():
            one.wait_send()
    for one in label_copies:
        one.wait_send()


def head(features, labels, weights, sampled):
    vmem = pl.BlockSpec(memory_space=pltpu.VMEM)
    dma = pltpu.SemaphoreType.DMA
    slots, column = NZ * NCORE, NYH * NYL
    scratch = [
        pltpu.VMEM((NZ, PAIR, WIDTH), jnp.bfloat16),
        pltpu.VMEM((2, BANKS, WIDTH), jnp.bfloat16),
        pltpu.VMEM((slots, 1, ROWS), jnp.int32),
        pltpu.VMEM((2, BANKS, PAIR), jnp.int32),
        pltpu.VMEM((2, NZ, BANKS, PAIR), jnp.float32),
        pltpu.VMEM((NZ, PAIR, PAIR), jnp.bfloat16),
        pltpu.VMEM((2, NZ, ROWS), jnp.float32),
        pltpu.VMEM((2, NZ, ROWS), jnp.float32),
        pltpu.VMEM((slots, 2, NZ, ROWS), jnp.float32),
        pltpu.VMEM((slots, 1, ROWS), jnp.float32),
        pltpu.VMEM((slots, 1, ROWS), jnp.float32),
        pltpu.VMEM((NX, PAIR, EAST), jnp.bfloat16),
        pltpu.VMEM((NX, PAIR, EAST), jnp.bfloat16),
        pltpu.VMEM((PAIR, EAST), jnp.float32),
        pltpu.VMEM((column, OUT_ROWS, EAST), jnp.bfloat16),
        pltpu.VMEM((column, OUT_ROWS, EAST), jnp.float32),
        pltpu.VMEM((column, OUT_ROWS, EAST), jnp.bfloat16),
        pltpu.VMEM((NX, column, OUT_ROWS, NORTH), jnp.bfloat16),
        pltpu.VMEM((NX, column, OUT_ROWS, NORTH), jnp.float32),
        pltpu.VMEM((NX, column, OUT_ROWS, NORTH), jnp.bfloat16),
        pltpu.VMEM((NX, OUT_ROWS, NORTH), jnp.bfloat16),
        pltpu.VMEM((NX, OUT_ROWS, NORTH), jnp.bfloat16),
        pltpu.VMEM((ROWS, WIDTH), jnp.bfloat16),
        pltpu.SMEM((PAIR,), jnp.int32),
        pltpu.VMEM((BANK, WIDTH), jnp.float32),
        pltpu.VMEM((ROWS, WIDTH), jnp.float32),
        dma((4,)),
    ]
    counts = (4 * NZ, 2 * NZ, slots, 4 * NX, slots, slots, 2 * NX, 2 * column, NX * column, NX)
    for count in counts:
        scratch += [dma((count,)), dma((count,))]
    return pl.pallas_call(
        head_kernel,
        out_shape=(
            jax.ShapeDtypeStruct((1, ROWS), jnp.float32),
            jax.ShapeDtypeStruct((OUT_ROWS, WIDTH), jnp.float32),
        ),
        in_specs=[pl.BlockSpec(memory_space=pltpu.HBM)] * 4,
        out_specs=(vmem, vmem),
        scratch_shapes=scratch,
        compiler_params=pltpu.CompilerParams(
            collective_id=0, has_side_effects=True, vmem_limit_bytes=55040 * 1024
        ),
    )(features, labels, weights, sampled)


def per_device(features, labels, weights, sampled):
    loss, grad = head(features, labels.reshape(1, ROWS), weights, sampled)
    return (loss.reshape(ROWS), grad)


def solution(mesh):
    in_specs = (P(("cls", "dp"), None), P(("cls", "dp")), P("cls", None), P("cls"))
    out_specs = (P(("cls", "dp")), P(("cls", "dp"), None))
    return jax.shard_map(
        per_device, mesh=mesh, in_specs=in_specs, out_specs=out_specs, check_vma=False
    )
```

```python
import functools

import jax
import jax.numpy as jnp
from jax import lax
from jax.experimental import pallas as pl
from jax.experimental.pallas import tpu as pltpu
from jax.sharding import PartitionSpec as P

logit_scale = 64.0
margin = 0.35
epsilon = 1e-06

NX, NZ, NYH, NYL, NCORE = 4, 8, 2, 4, 2
ROWS = 128
OUT_ROWS = 32
BANK = 1024
WIDTH = 512
PAIR = 2 * ROWS
HALF = ROWS // 2
QUARTER = ROWS // 4
BANKS = NX * ROWS
EAST = 384
NORTH = WIDTH - EAST
EAST_CUTS = ((0, 256), (256, 128))


def normalize_rows(matrix):
    squares = jnp.sum(matrix * matrix, axis=1, keepdims=True)
    return lax.rsqrt(squares + epsilon)


def head_kernel(
    feat_ref,
    label_ref,
    bank_ref,
    sampled_ref,
    loss_ref,
    grad_ref,
    feats,
    classes,
    labels,
    ids,
    probs,
    grads,
    inverse_total,
    sums,
    sums_in,
    targets,
    targets_in,
    part_out,
    part_in,
    part_own,
    half_out,
    half_own,
    half_in,
    north_out,
    north_own,
    north_in,
    last_out,
    last_in,
    feat_in,
    places,
    bank,
    chosen,
    load_sem,
    feat_send,
    feat_recv,
    core_send,
    core_recv,
    label_send,
    label_recv,
    class_send,
    class_recv,
    sum_send,
    sum_recv,
    target_send,
    target_recv,
    part_send,
    part_recv,
    half_send,
    half_recv,
    north_send,
    north_recv,
    last_send,
    last_recv,
):
    cls, dp = lax.axis_index("cls"), lax.axis_index("dp")
    x, z, yh = lax.div(cls, 16), lax.rem(lax.div(cls, 2), 8), lax.rem(cls, 2)
    yl, core = lax.div(dp, 2), lax.rem(dp, 2)

    def device(dx=0, dz=0, dyh=0, dyl=0, dcore=0):
        px = lax.rem(x + dx, NX)
        pz = lax.rem(z + dz, NZ)
        pyh = lax.rem(yh + dyh, NYH)
        pyl = lax.rem(yl + dyl, NYL)
        pcore = lax.rem(core + dcore, NCORE)
        return ((px * NZ + pz) * NYH + pyh, pyl * NCORE + pcore)

    mirror = ((x * NZ + z) * NYH + (1 - yh), (NYL - 1 - yl) * NCORE + core)

    def copy(src, dst, send, recv, target):
        return pltpu.make_async_remote_copy(
            src_ref=src,
            dst_ref=dst,
            send_sem=send,
            recv_sem=recv,
            device_id=target,
            device_id_type=pl.DeviceIdType.MESH,
        )

    plane = [(o, w) for o in range(NZ) for w in range(NCORE) if (o, w) != (0, 0)]
    column = [(u, v) for u in range(NYH) for v in range(NYL) if (u, v) != (0, 0)]

    feat_load = pltpu.make_async_copy(feat_ref, feat_in, load_sem.at[0])
    label_load = pltpu.make_async_copy(label_ref, labels.at[0], load_sem.at[1])
    sampled_load = pltpu.make_async_copy(sampled_ref, places, load_sem.at[2])
    bank_load = pltpu.make_async_copy(bank_ref, bank, load_sem.at[3])
    for one in (feat_load, label_load, sampled_load, bank_load):
        one.start()
    barrier = pltpu.get_barrier_semaphore()
    peers = [device(dz=o, dcore=w) for o, w in plane]
    peers += [device(dx=i) for i in range(1, NX)]
    peers += [device(dyh=u, dyl=v) for u, v in column]
    for peer in peers:
        pl.semaphore_signal(barrier, inc=1, device_id=peer, device_id_type=pl.DeviceIdType.MESH)
    feat_load.wait()
    feat_wide = feat_in[...].astype(jnp.float32)
    feats[0, :ROWS] = (feat_wide * normalize_rows(feat_wide)).astype(jnp.bfloat16)
    label_load.wait()
    sums[...] = jnp.zeros_like(sums)
    targets[...] = jnp.zeros_like(targets)
    pl.semaphore_wait(barrier, len(peers))

    def feat_copy(slot, h):
        if slot < NZ // 2 or (slot == NZ // 2 and h < 2):
            came, target = slot - 1, device(dz=1)
        else:
            came, target = (slot + 1) % NZ, device(dz=NZ - 1)
        rows = pl.ds(h * QUARTER, QUARTER)
        k = 4 * slot + h
        return copy(
            feats.at[came, rows], feats.at[slot, rows], feat_send.at[k], feat_recv.at[k], target
        )

    def core_copy(slot, h):
        rows = pl.ds(h * HALF, HALF)
        k = 2 * slot + h
        return copy(
            feats.at[slot, rows],
            feats.at[slot, pl.ds(ROWS + h * HALF, HALF)],
            core_send.at[k],
            core_recv.at[k],
            device(dcore=1),
        )

    def class_copy(i, u, h):
        rows = pl.ds(i * ROWS + h * HALF, HALF)
        near = pl.ds(h * HALF, HALF)
        if i == 0:
            target = mirror
        else:
            target = device(dx=i)
        k = 4 * i + 2 * u + h
        src = classes.at[1 if i and u else 0, near]
        return copy(src, classes.at[u, rows], class_send.at[k], class_recv.at[k], target)

    def label_copy(o, w):
        k = 2 * o + w
        return copy(
            labels.at[0], labels.at[k], label_send.at[k], label_recv.at[k], device(dz=o, dcore=w)
        )

    feat_copies = {(s, h): feat_copy(s, h) for s in range(1, NZ) for h in range(4)}
    core_copies = {(s, h): core_copy(s, h) for s in range(NZ) for h in range(2)}
    class_copies = {
        (i, u, h): class_copy(i, u, h)
        for i in range(NX)
        for u in range(2)
        for h in range(2)
        if i + u
    }
    label_copies = [label_copy(o, w) for o, w in plane]

    for h in range(4):
        feat_copies[1, h].start()
        feat_copies[NZ - 1, h].start()
    for h in range(2):
        core_copies[0, h].start()
    for one in label_copies:
        one.start()

    sampled_load.wait()
    bank_load.wait()

    @pl.loop(0, ROWS // 8)
    def _(block):
        for r in range(8):
            k = block * 8 + r
            place = lax.div(k, OUT_ROWS) * (2 * OUT_ROWS) + core * OUT_ROWS + lax.rem(k, OUT_ROWS)
            chosen[pl.ds(k, 1)] = bank[pl.ds(places[place], 1)]

    picked = chosen[...]
    classes[0, :ROWS] = (picked * normalize_rows(picked)).astype(jnp.bfloat16)
    row = lax.broadcasted_iota(jnp.int32, (ROWS, PAIR), 0)
    within = (
        lax.shift_right_logical(row, 5) * (2 * OUT_ROWS)
        + lax.bitwise_and(row, OUT_ROWS - 1)
        + (z * (2 * PAIR) + core * OUT_ROWS)
    )
    for i in range(NX):
        base = lax.rem(x + (NX - i), NX) * (NZ * NYH * PAIR)
        ids[0, i * ROWS : (i + 1) * ROWS] = within + (base + yh * PAIR)
        ids[1, i * ROWS : (i + 1) * ROWS] = within + (base + (1 - yh) * PAIR)
    for h in range(2):
        class_copies[0, 1, h].start()
    for i in (2, 1, 3):
        for h in range(2):
            class_copies[i, 0, h].start()

    def names(s):
        return jnp.concatenate([labels[2 * s], labels[2 * s + 1]], axis=1)

    def first_pass(s, u):
        cosine = lax.dot_general(
            classes[u],
            feats[s],
            (((1,), (1,)), ((), ())),
            preferred_element_type=jnp.float32,
        )
        hit = ids[u] == names(s)
        logits = logit_scale * (cosine - jnp.where(hit, margin, 0.0))
        prob = jnp.exp(logits - logit_scale)
        probs[u, s] = prob
        total = jnp.sum(prob, axis=0, keepdims=True)
        target = jnp.sum(jnp.where(hit, logits, 0.0), axis=0, keepdims=True)
        sums[0, pl.ds(s, 1)] += total[:, :ROWS]
        sums[1, pl.ds(s, 1)] += total[:, ROWS:]
        targets[2 * s] += target[:, :ROWS]
        targets[2 * s + 1] += target[:, ROWS:]

    def receive_features(step):
        back = NZ - step
        for h in range(4):
            if step < NZ // 2:
                feat_copies[step, h].wait_recv()
                if step + 1 < NZ // 2 or h < 2:
                    feat_copies[step + 1, h].start()
                feat_copies[back, h].wait_recv()
                if step + 1 < NZ // 2 or h >= 2:
                    feat_copies[back - 1, h].start()
                if h % 2:
                    core_copies[step, h // 2].start()
                    core_copies[back, h // 2].start()
            if step == 2 and h % 2:
                class_copies[0, 1, h // 2].wait_recv()
                for i in (2, 1, 3):
                    class_copies[i, 1, h // 2].start()
        if step == NZ // 2:
            for h in (0, 2, 1, 3):
                feat_copies[step, h].wait_recv()
                if h in (1, 3):
                    core_copies[step, h // 2].start()

    def receive_cores(*slots):
        for slot in slots:
            for h in range(2):
                core_copies[slot, h].wait_recv()

    def receive_classes(u):
        for i in range(1, NX):
            for h in range(2):
                class_copies[i, u, h].wait_recv()

    receive_features(1)
    receive_features(2)
    receive_classes(0)
    for one in label_copies:
        one.wait_recv()
    receive_cores(0, 1, 7)

    @pl.loop(0, 3)
    def _(k):
        first_pass(lax.rem(k + (NZ - 1), NZ), 0)

    receive_features(3)
    receive_cores(2, 6, 3, 5)

    @pl.loop(0, 4)
    def _(k):
        first_pass(2 + lax.div(k, 2) + lax.rem(k, 2) * (NZ - 4 - 2 * lax.div(k, 2)), 0)

    receive_classes(1)

    @pl.loop(0, 3)
    def _(k):
        first_pass(lax.rem(k + (NZ - 1), NZ), 1)

    receive_features(4)

    @pl.loop(0, 4)
    def _(k):
        first_pass(2 + lax.div(k, 2) + lax.rem(k, 2) * (NZ - 4 - 2 * lax.div(k, 2)), 1)

    receive_cores(4)

    @pl.loop(0, 2)
    def _(k):
        first_pass(NZ // 2, k)

    sum_copies, target_copies = {}, {}
    for o, w in plane:
        k = 2 * o + w
        sum_copies[o, w] = copy(
            sums, sums_in.at[k], sum_send.at[k], sum_recv.at[k], device(dz=o, dcore=w)
        )
        target_copies[o, w] = copy(
            targets.at[k],
            targets_in.at[k],
            target_send.at[k],
            target_recv.at[k],
            device(dz=NZ - o, dcore=w),
        )
    for one in sum_copies.values():
        one.start()
    for one in target_copies.values():
        one.start()
    whole = [sums[0], sums[1]]
    for (o, w), one in sum_copies.items():
        one.wait_recv()
        for q in range(2):
            other = sums_in[2 * o + w, (q + w) % 2]
            whole[q] += other if o == 0 else pltpu.roll(other, o, 0)
    for q in range(2):
        inverse_total[q] = 1.0 / whole[q]

    part_copies, north_copies = {}, {}

    def send_part(turn, i):
        columns = pl.ds(*EAST_CUTS[turn])
        part_copies[turn, i] = copy(
            part_out.at[i, :, columns],
            part_in.at[i, :, columns],
            part_send.at[NX * turn + i],
            part_recv.at[NX * turn + i],
            device(dx=NX - i),
        )
        part_copies[turn, i].start()

    for i in (2, 1, 3, 0):

        def weigh(s, carry):
            inverse = jnp.concatenate(
                [inverse_total[0, pl.ds(s, 1)], inverse_total[1, pl.ds(s, 1)]], axis=1
            )
            name = names(s)
            for u in range(2):
                rows = pl.ds(i * ROWS, ROWS)
                hit = jnp.where(ids[u, rows] == name, 1.0, 0.0)
                slope = probs[u, s, rows] * inverse - hit
                grads[s, u * ROWS : (u + 1) * ROWS] = slope.astype(jnp.bfloat16)
            return carry

        lax.fori_loop(0, NZ, weigh, 0)
        part = jnp.zeros((PAIR, WIDTH), jnp.float32)
        for s in range(NZ):
            part += jnp.dot(grads[s], feats[s], preferred_element_type=jnp.float32)
        north = part[:, EAST:].reshape(NYH * NYL, OUT_ROWS, NORTH)
        north_own[i] = north
        north_out[i] = north.astype(jnp.bfloat16)
        if i == 0:
            part_own[...] = part[:, :EAST]
        else:
            part_out[i] = part[:, :EAST].astype(jnp.bfloat16)
            send_part(0, i)
        for u, v in column:
            k = NYL * u + v
            north_copies[i, k] = copy(
                north_out.at[i, NYL * u + lax.rem(yl + v, NYL)],
                north_in.at[i, k],
                north_send.at[NX * k + i],
                north_recv.at[NX * k + i],
                device(dyh=u, dyl=v),
            )
            north_copies[i, k].start()

    for i in (2, 1, 3):
        send_part(1, i)

    own_target = targets[0]
    for (o, w), one in target_copies.items():
        one.wait_recv()
        own_target += targets_in[2 * o + w]
    loss_ref[...] = logit_scale + jnp.log(whole[0][0:1]) - own_target

    last_copies = {}
    for i in (2, 1, 3, 0):
        north = north_own[i, yl]
        for k in range(1, NYH * NYL):
            north_copies[i, k].wait_recv()
            north += north_in[i, k].astype(jnp.float32)
        if i > 0:
            last_out[i] = north.astype(jnp.bfloat16)
            last_copies[i] = copy(
                last_out.at[i],
                last_in.at[i],
                last_send.at[i],
                last_recv.at[i],
                device(dx=NX - i),
            )
            last_copies[i].start()

    half_copies = {}
    for turn, (start, width) in enumerate(EAST_CUTS):
        columns = slice(start, start + width)
        half = part_own[:, columns]
        for i in (1, 3, 2):
            part_copies[turn, i].wait_recv()
            half += part_in[i, :, columns].astype(jnp.float32)
        half = half.reshape(NYH * NYL, OUT_ROWS, width)
        half_own[:, :, columns] = half
        half_out[:, :, columns] = half.astype(jnp.bfloat16)
        for u, v in column:
            k = NYL * u + v
            half_copies[turn, k] = copy(
                half_out.at[NYL * u + lax.rem(yl + v, NYL), :, pl.ds(start, width)],
                half_in.at[k, :, pl.ds(start, width)],
                half_send.at[NYH * NYL * turn + k],
                half_recv.at[NYH * NYL * turn + k],
                device(dyh=u, dyl=v),
            )
            half_copies[turn, k].start()
    for i, one in last_copies.items():
        one.wait_recv()
        north += last_in[i].astype(jnp.float32)
    pieces = []
    for turn, (start, width) in enumerate(EAST_CUTS):
        columns = slice(start, start + width)
        piece = half_own[yl, :, columns]
        for k in range(1, NYH * NYL):
            half_copies[turn, k].wait_recv()
            piece += half_in[k, :, columns].astype(jnp.float32)
        pieces.append(piece)
    pieces.append(north)
    total = (logit_scale / 8.0) * jnp.concatenate(pieces, axis=1)
    own = chosen[pl.ds(pl.multiple_of(yl * OUT_ROWS, OUT_ROWS), OUT_ROWS)]
    inverse = normalize_rows(own)
    unit = own * inverse
    radial = jnp.sum(unit * total, axis=1, keepdims=True)
    grad_ref[...] = inverse * (total - unit * radial)

    for group in (
        feat_copies,
        core_copies,
        class_copies,
        sum_copies,
        target_copies,
        part_copies,
        half_copies,
        north_copies,
        last_copies,
    ):
        for one in group.values():
            one.wait_send()
    for one in label_copies:
        one.wait_send()


def head(features, labels, weights, sampled):
    vmem = pl.BlockSpec(memory_space=pltpu.VMEM)
    operands = [
        pltpu.with_memory_space_constraint(one, pltpu.HBM)
        for one in (features, labels, weights, sampled)
    ]
    dma = pltpu.SemaphoreType.DMA
    slots, column = NZ * NCORE, NYH * NYL
    scratch = [
        pltpu.VMEM((NZ, PAIR, WIDTH), jnp.bfloat16),
        pltpu.VMEM((2, BANKS, WIDTH), jnp.bfloat16),
        pltpu.VMEM((slots, 1, ROWS), jnp.int32),
        pltpu.VMEM((2, BANKS, PAIR), jnp.int32),
        pltpu.VMEM((2, NZ, BANKS, PAIR), jnp.float32),
        pltpu.VMEM((NZ, PAIR, PAIR), jnp.bfloat16),
        pltpu.VMEM((2, NZ, ROWS), jnp.float32),
        pltpu.VMEM((2, NZ, ROWS), jnp.float32),
        pltpu.VMEM((slots, 2, NZ, ROWS), jnp.float32),
        pltpu.VMEM((slots, 1, ROWS), jnp.float32),
        pltpu.VMEM((slots, 1, ROWS), jnp.float32),
        pltpu.VMEM((NX, PAIR, EAST), jnp.bfloat16),
        pltpu.VMEM((NX, PAIR, EAST), jnp.bfloat16),
        pltpu.VMEM((PAIR, EAST), jnp.float32),
        pltpu.VMEM((column, OUT_ROWS, EAST), jnp.bfloat16),
        pltpu.VMEM((column, OUT_ROWS, EAST), jnp.float32),
        pltpu.VMEM((column, OUT_ROWS, EAST), jnp.bfloat16),
        pltpu.VMEM((NX, column, OUT_ROWS, NORTH), jnp.bfloat16),
        pltpu.VMEM((NX, column, OUT_ROWS, NORTH), jnp.float32),
        pltpu.VMEM((NX, column, OUT_ROWS, NORTH), jnp.bfloat16),
        pltpu.VMEM((NX, OUT_ROWS, NORTH), jnp.bfloat16),
        pltpu.VMEM((NX, OUT_ROWS, NORTH), jnp.bfloat16),
        pltpu.VMEM((ROWS, WIDTH), jnp.bfloat16),
        pltpu.SMEM((PAIR,), jnp.int32),
        pltpu.VMEM((BANK, WIDTH), jnp.float32),
        pltpu.VMEM((ROWS, WIDTH), jnp.float32),
        dma((4,)),
    ]
    counts = (4 * NZ, 2 * NZ, slots, 4 * NX, slots, slots, 2 * NX, 2 * column, NX * column, NX)
    for count in counts:
        scratch += [dma((count,)), dma((count,))]
    return pl.pallas_call(
        head_kernel,
        out_shape=(
            jax.ShapeDtypeStruct((1, ROWS), jnp.float32),
            jax.ShapeDtypeStruct((OUT_ROWS, WIDTH), jnp.float32),
        ),
        in_specs=[pl.BlockSpec(memory_space=pltpu.HBM)] * 4,
        out_specs=(vmem, vmem),
        scratch_shapes=scratch,
        compiler_params=pltpu.CompilerParams(
            collective_id=0, has_side_effects=True, vmem_limit_bytes=48 * 1024 * 1024
        ),
    )(*operands)


def per_device(features, labels, weights, sampled):
    loss, grad = head(features, labels.reshape(1, ROWS), weights, sampled)
    return (loss.reshape(ROWS), grad)


def solution(mesh):
    in_specs = (P(("cls", "dp"), None), P(("cls", "dp")), P("cls", None), P("cls"))
    out_specs = (P(("cls", "dp")), P(("cls", "dp"), None))
    return jax.shard_map(
        per_device, mesh=mesh, in_specs=in_specs, out_specs=out_specs, check_vma=False
    )
```

```python
import functools

import jax
import jax.numpy as jnp
from jax import lax
from jax.experimental import pallas as pl
from jax.experimental.pallas import tpu as pltpu
from jax.sharding import PartitionSpec as P

logit_scale = 64.0
margin = 0.35
epsilon = 1e-06

NX, NZ, NYH, NYL, NCORE = 4, 8, 2, 4, 2
ROWS = 128
OUT_ROWS = 32
BANK = 1024
WIDTH = 512
PAIR = 2 * ROWS
HALF = ROWS // 2
QUARTER = ROWS // 4
BANKS = NX * ROWS
EAST = 384
NORTH = WIDTH - EAST
EAST_CUTS = ((0, 256), (256, 128))


def normalize_rows(matrix):
    squares = jnp.sum(matrix * matrix, axis=1, keepdims=True)
    return lax.rsqrt(squares + epsilon)


def head_kernel(
    feat_ref,
    label_ref,
    bank_ref,
    sampled_ref,
    loss_ref,
    grad_ref,
    feats,
    classes,
    labels,
    ids,
    probs,
    grads,
    inverse_total,
    sums,
    sums_in,
    targets,
    targets_in,
    part_out,
    part_in,
    part_own,
    half_out,
    half_own,
    half_in,
    north_out,
    north_own,
    north_in,
    last_out,
    last_in,
    feat_in,
    places,
    bank,
    chosen,
    load_sem,
    feat_send,
    feat_recv,
    core_send,
    core_recv,
    label_send,
    label_recv,
    class_send,
    class_recv,
    sum_send,
    sum_recv,
    target_send,
    target_recv,
    part_send,
    part_recv,
    half_send,
    half_recv,
    north_send,
    north_recv,
    last_send,
    last_recv,
):
    cls, dp = lax.axis_index("cls"), lax.axis_index("dp")
    x, z, yh = lax.div(cls, 16), lax.rem(lax.div(cls, 2), 8), lax.rem(cls, 2)
    yl, core = lax.div(dp, 2), lax.rem(dp, 2)

    def device(dx=0, dz=0, dyh=0, dyl=0, dcore=0):
        px = lax.rem(x + dx, NX)
        pz = lax.rem(z + dz, NZ)
        pyh = lax.rem(yh + dyh, NYH)
        pyl = lax.rem(yl + dyl, NYL)
        pcore = lax.rem(core + dcore, NCORE)
        return ((px * NZ + pz) * NYH + pyh, pyl * NCORE + pcore)

    mirror = ((x * NZ + z) * NYH + (1 - yh), (NYL - 1 - yl) * NCORE + core)

    def copy(src, dst, send, recv, target):
        return pltpu.make_async_remote_copy(
            src_ref=src,
            dst_ref=dst,
            send_sem=send,
            recv_sem=recv,
            device_id=target,
            device_id_type=pl.DeviceIdType.MESH,
        )

    plane = [(o, w) for o in range(NZ) for w in range(NCORE) if (o, w) != (0, 0)]
    column = [(u, v) for u in range(NYH) for v in range(NYL) if (u, v) != (0, 0)]

    feat_load = pltpu.make_async_copy(feat_ref, feat_in, load_sem.at[0])
    label_load = pltpu.make_async_copy(label_ref, labels.at[0], load_sem.at[1])
    sampled_load = pltpu.make_async_copy(sampled_ref, places, load_sem.at[2])
    bank_load = pltpu.make_async_copy(bank_ref, bank, load_sem.at[3])
    for one in (feat_load, label_load, sampled_load, bank_load):
        one.start()
    barrier = pltpu.get_barrier_semaphore()
    peers = [device(dz=o, dcore=w) for o, w in plane]
    peers += [device(dx=i) for i in range(1, NX)]
    peers += [device(dyh=u, dyl=v) for u, v in column]
    for peer in peers:
        pl.semaphore_signal(barrier, inc=1, device_id=peer, device_id_type=pl.DeviceIdType.MESH)
    feat_load.wait()
    feat_wide = feat_in[...].astype(jnp.float32)
    feats[0, :ROWS] = (feat_wide * normalize_rows(feat_wide)).astype(jnp.bfloat16)
    label_load.wait()
    sums[...] = jnp.zeros_like(sums)
    targets[...] = jnp.zeros_like(targets)
    pl.semaphore_wait(barrier, len(peers))

    def feat_copy(slot, h):
        if slot < NZ // 2 or (slot == NZ // 2 and h < 2):
            came, target = slot - 1, device(dz=1)
        else:
            came, target = (slot + 1) % NZ, device(dz=NZ - 1)
        rows = pl.ds(h * QUARTER, QUARTER)
        k = 4 * slot + h
        return copy(
            feats.at[came, rows], feats.at[slot, rows], feat_send.at[k], feat_recv.at[k], target
        )

    def core_copy(slot, h):
        rows = pl.ds(h * HALF, HALF)
        k = 2 * slot + h
        return copy(
            feats.at[slot, rows],
            feats.at[slot, pl.ds(ROWS + h * HALF, HALF)],
            core_send.at[k],
            core_recv.at[k],
            device(dcore=1),
        )

    def class_copy(i, u, h):
        rows = pl.ds(i * ROWS + h * HALF, HALF)
        near = pl.ds(h * HALF, HALF)
        if i == 0:
            target = mirror
        else:
            target = device(dx=i)
        k = 4 * i + 2 * u + h
        src = classes.at[1 if i and u else 0, near]
        return copy(src, classes.at[u, rows], class_send.at[k], class_recv.at[k], target)

    def label_copy(o, w):
        k = 2 * o + w
        return copy(
            labels.at[0], labels.at[k], label_send.at[k], label_recv.at[k], device(dz=o, dcore=w)
        )

    feat_copies = {(s, h): feat_copy(s, h) for s in range(1, NZ) for h in range(4)}
    core_copies = {(s, h): core_copy(s, h) for s in range(NZ) for h in range(2)}
    class_copies = {
        (i, u, h): class_copy(i, u, h)
        for i in range(NX)
        for u in range(2)
        for h in range(2)
        if i + u
    }
    label_copies = [label_copy(o, w) for o, w in plane]

    for h in range(4):
        feat_copies[1, h].start()
        feat_copies[NZ - 1, h].start()
    for h in range(2):
        core_copies[0, h].start()
    for one in label_copies:
        one.start()

    sampled_load.wait()
    bank_load.wait()

    @pl.loop(0, ROWS // 8)
    def _(block):
        for r in range(8):
            k = block * 8 + r
            place = lax.div(k, OUT_ROWS) * (2 * OUT_ROWS) + core * OUT_ROWS + lax.rem(k, OUT_ROWS)
            chosen[pl.ds(k, 1)] = bank[pl.ds(places[place], 1)]

    picked = chosen[...]
    classes[0, :ROWS] = (picked * normalize_rows(picked)).astype(jnp.bfloat16)
    row = lax.broadcasted_iota(jnp.int32, (ROWS, PAIR), 0)
    within = (
        lax.shift_right_logical(row, 5) * (2 * OUT_ROWS)
        + lax.bitwise_and(row, OUT_ROWS - 1)
        + (z * (2 * PAIR) + core * OUT_ROWS)
    )
    for i in range(NX):
        base = lax.rem(x + (NX - i), NX) * (NZ * NYH * PAIR)
        ids[0, i * ROWS : (i + 1) * ROWS] = within + (base + yh * PAIR)
        ids[1, i * ROWS : (i + 1) * ROWS] = within + (base + (1 - yh) * PAIR)
    for h in range(2):
        class_copies[0, 1, h].start()
    for i in (2, 1, 3):
        for h in range(2):
            class_copies[i, 0, h].start()

    def names(s):
        return jnp.concatenate([labels[2 * s], labels[2 * s + 1]], axis=1)

    def first_pass(s, u):
        cosine = lax.dot_general(
            classes[u],
            feats[s],
            (((1,), (1,)), ((), ())),
            preferred_element_type=jnp.float32,
        )
        hit = ids[u] == names(s)
        logits = logit_scale * (cosine - jnp.where(hit, margin, 0.0))
        prob = jnp.exp(logits - logit_scale)
        probs[u, s] = prob
        total = jnp.sum(prob, axis=0, keepdims=True)
        target = jnp.sum(jnp.where(hit, logits, 0.0), axis=0, keepdims=True)
        sums[0, pl.ds(s, 1)] += total[:, :ROWS]
        sums[1, pl.ds(s, 1)] += total[:, ROWS:]
        targets[2 * s] += target[:, :ROWS]
        targets[2 * s + 1] += target[:, ROWS:]

    def forward_classes(h):
        class_copies[0, 1, h].wait_recv()
        for i in (2, 1, 3):
            class_copies[i, 1, h].start()

    def receive_features(step):
        back = NZ - step
        for h in range(4):
            if step < NZ // 2:
                feat_copies[step, h].wait_recv()
                if step + 1 < NZ // 2 or h < 2:
                    feat_copies[step + 1, h].start()
                feat_copies[back, h].wait_recv()
                if step + 1 < NZ // 2 or h >= 2:
                    feat_copies[back - 1, h].start()
                if h % 2:
                    core_copies[step, h // 2].start()
                    core_copies[back, h // 2].start()
            if step == 3 and h == 1:
                forward_classes(1)
        if step == NZ // 2:
            for h in (0, 2, 1, 3):
                feat_copies[step, h].wait_recv()
                if h in (1, 3):
                    core_copies[step, h // 2].start()

    def receive_cores(*slots):
        for slot in slots:
            for h in range(2):
                core_copies[slot, h].wait_recv()

    def receive_classes(u):
        for i in range(1, NX):
            for h in range(2):
                class_copies[i, u, h].wait_recv()

    receive_features(1)
    receive_features(2)
    forward_classes(0)
    receive_features(3)
    receive_classes(0)
    for one in label_copies:
        one.wait_recv()
    receive_cores(0, 1, 7)

    @pl.loop(0, 3)
    def _(k):
        first_pass(lax.rem(k + (NZ - 1), NZ), 0)

    receive_cores(2, 6, 3, 5)

    @pl.loop(0, 4)
    def _(k):
        first_pass(2 + lax.div(k, 2) + lax.rem(k, 2) * (NZ - 4 - 2 * lax.div(k, 2)), 0)

    receive_classes(1)

    @pl.loop(0, 3)
    def _(k):
        first_pass(lax.rem(k + (NZ - 1), NZ), 1)

    receive_features(4)

    @pl.loop(0, 4)
    def _(k):
        first_pass(2 + lax.div(k, 2) + lax.rem(k, 2) * (NZ - 4 - 2 * lax.div(k, 2)), 1)

    receive_cores(4)

    @pl.loop(0, 2)
    def _(k):
        first_pass(NZ // 2, k)

    sum_copies, target_copies = {}, {}
    for o, w in plane:
        k = 2 * o + w
        sum_copies[o, w] = copy(
            sums, sums_in.at[k], sum_send.at[k], sum_recv.at[k], device(dz=o, dcore=w)
        )
        target_copies[o, w] = copy(
            targets.at[k],
            targets_in.at[k],
            target_send.at[k],
            target_recv.at[k],
            device(dz=NZ - o, dcore=w),
        )
    for one in sum_copies.values():
        one.start()
    for one in target_copies.values():
        one.start()
    whole = [sums[0], sums[1]]
    for (o, w), one in sum_copies.items():
        one.wait_recv()
        for q in range(2):
            other = sums_in[2 * o + w, (q + w) % 2]
            whole[q] += other if o == 0 else pltpu.roll(other, o, 0)
    for q in range(2):
        inverse_total[q] = 1.0 / whole[q]

    part_copies, north_copies = {}, {}

    def send_part(turn, i):
        columns = pl.ds(*EAST_CUTS[turn])
        part_copies[turn, i] = copy(
            part_out.at[i, :, columns],
            part_in.at[i, :, columns],
            part_send.at[NX * turn + i],
            part_recv.at[NX * turn + i],
            device(dx=NX - i),
        )
        part_copies[turn, i].start()

    for i in (2, 1, 3, 0):

        def weigh(s, carry):
            inverse = jnp.concatenate(
                [inverse_total[0, pl.ds(s, 1)], inverse_total[1, pl.ds(s, 1)]], axis=1
            )
            name = names(s)
            for u in range(2):
                rows = pl.ds(i * ROWS, ROWS)
                hit = jnp.where(ids[u, rows] == name, 1.0, 0.0)
                slope = probs[u, s, rows] * inverse - hit
                grads[s, u * ROWS : (u + 1) * ROWS] = slope.astype(jnp.bfloat16)
            return carry

        lax.fori_loop(0, NZ, weigh, 0)
        part = jnp.zeros((PAIR, WIDTH), jnp.float32)
        for s in range(NZ):
            part += jnp.dot(grads[s], feats[s], preferred_element_type=jnp.float32)
        north = part[:, EAST:].reshape(NYH * NYL, OUT_ROWS, NORTH)
        north_own[i] = north
        north_out[i] = north.astype(jnp.bfloat16)
        if i == 0:
            part_own[...] = part[:, :EAST]
        else:
            part_out[i] = part[:, :EAST].astype(jnp.bfloat16)
            send_part(0, i)
        for u, v in column:
            k = NYL * u + v
            north_copies[i, k] = copy(
                north_out.at[i, NYL * u + lax.rem(yl + v, NYL)],
                north_in.at[i, k],
                north_send.at[NX * k + i],
                north_recv.at[NX * k + i],
                device(dyh=u, dyl=v),
            )
            north_copies[i, k].start()

    for i in (2, 1, 3):
        send_part(1, i)

    own_target = targets[0]
    for (o, w), one in target_copies.items():
        one.wait_recv()
        own_target += targets_in[2 * o + w]
    loss_ref[...] = logit_scale + jnp.log(whole[0][0:1]) - own_target

    last_copies = {}
    for i in (2, 1, 3, 0):
        north = north_own[i, yl]
        for k in range(1, NYH * NYL):
            north_copies[i, k].wait_recv()
            north += north_in[i, k].astype(jnp.float32)
        if i > 0:
            last_out[i] = north.astype(jnp.bfloat16)
            last_copies[i] = copy(
                last_out.at[i],
                last_in.at[i],
                last_send.at[i],
                last_recv.at[i],
                device(dx=NX - i),
            )
            last_copies[i].start()

    half_copies = {}
    for turn, (start, width) in enumerate(EAST_CUTS):
        columns = slice(start, start + width)
        half = part_own[:, columns]
        for i in (1, 3, 2):
            part_copies[turn, i].wait_recv()
            half += part_in[i, :, columns].astype(jnp.float32)
        half = half.reshape(NYH * NYL, OUT_ROWS, width)
        half_own[:, :, columns] = half
        half_out[:, :, columns] = half.astype(jnp.bfloat16)
        for u, v in column:
            k = NYL * u + v
            half_copies[turn, k] = copy(
                half_out.at[NYL * u + lax.rem(yl + v, NYL), :, pl.ds(start, width)],
                half_in.at[k, :, pl.ds(start, width)],
                half_send.at[NYH * NYL * turn + k],
                half_recv.at[NYH * NYL * turn + k],
                device(dyh=u, dyl=v),
            )
            half_copies[turn, k].start()
    for i, one in last_copies.items():
        one.wait_recv()
        north += last_in[i].astype(jnp.float32)
    pieces = []
    for turn, (start, width) in enumerate(EAST_CUTS):
        columns = slice(start, start + width)
        piece = half_own[yl, :, columns]
        for k in range(1, NYH * NYL):
            half_copies[turn, k].wait_recv()
            piece += half_in[k, :, columns].astype(jnp.float32)
        pieces.append(piece)
    pieces.append(north)
    total = (logit_scale / 8.0) * jnp.concatenate(pieces, axis=1)
    own = chosen[pl.ds(pl.multiple_of(yl * OUT_ROWS, OUT_ROWS), OUT_ROWS)]
    inverse = normalize_rows(own)
    unit = own * inverse
    radial = jnp.sum(unit * total, axis=1, keepdims=True)
    grad_ref[...] = inverse * (total - unit * radial)

    for group in (
        feat_copies,
        core_copies,
        class_copies,
        sum_copies,
        target_copies,
        part_copies,
        half_copies,
        north_copies,
        last_copies,
    ):
        for one in group.values():
            one.wait_send()
    for one in label_copies:
        one.wait_send()


def head(features, labels, weights, sampled):
    vmem = pl.BlockSpec(memory_space=pltpu.VMEM)
    operands = [
        pltpu.with_memory_space_constraint(one, pltpu.HBM)
        for one in (features, labels, weights, sampled)
    ]
    dma = pltpu.SemaphoreType.DMA
    slots, column = NZ * NCORE, NYH * NYL
    scratch = [
        pltpu.VMEM((NZ, PAIR, WIDTH), jnp.bfloat16),
        pltpu.VMEM((2, BANKS, WIDTH), jnp.bfloat16),
        pltpu.VMEM((slots, 1, ROWS), jnp.int32),
        pltpu.VMEM((2, BANKS, PAIR), jnp.int32),
        pltpu.VMEM((2, NZ, BANKS, PAIR), jnp.float32),
        pltpu.VMEM((NZ, PAIR, PAIR), jnp.bfloat16),
        pltpu.VMEM((2, NZ, ROWS), jnp.float32),
        pltpu.VMEM((2, NZ, ROWS), jnp.float32),
        pltpu.VMEM((slots, 2, NZ, ROWS), jnp.float32),
        pltpu.VMEM((slots, 1, ROWS), jnp.float32),
        pltpu.VMEM((slots, 1, ROWS), jnp.float32),
        pltpu.VMEM((NX, PAIR, EAST), jnp.bfloat16),
        pltpu.VMEM((NX, PAIR, EAST), jnp.bfloat16),
        pltpu.VMEM((PAIR, EAST), jnp.float32),
        pltpu.VMEM((column, OUT_ROWS, EAST), jnp.bfloat16),
        pltpu.VMEM((column, OUT_ROWS, EAST), jnp.float32),
        pltpu.VMEM((column, OUT_ROWS, EAST), jnp.bfloat16),
        pltpu.VMEM((NX, column, OUT_ROWS, NORTH), jnp.bfloat16),
        pltpu.VMEM((NX, column, OUT_ROWS, NORTH), jnp.float32),
        pltpu.VMEM((NX, column, OUT_ROWS, NORTH), jnp.bfloat16),
        pltpu.VMEM((NX, OUT_ROWS, NORTH), jnp.bfloat16),
        pltpu.VMEM((NX, OUT_ROWS, NORTH), jnp.bfloat16),
        pltpu.VMEM((ROWS, WIDTH), jnp.bfloat16),
        pltpu.SMEM((PAIR,), jnp.int32),
        pltpu.VMEM((BANK, WIDTH), jnp.float32),
        pltpu.VMEM((ROWS, WIDTH), jnp.float32),
        dma((4,)),
    ]
    counts = (4 * NZ, 2 * NZ, slots, 4 * NX, slots, slots, 2 * NX, 2 * column, NX * column, NX)
    for count in counts:
        scratch += [dma((count,)), dma((count,))]
    return pl.pallas_call(
        head_kernel,
        out_shape=(
            jax.ShapeDtypeStruct((1, ROWS), jnp.float32),
            jax.ShapeDtypeStruct((OUT_ROWS, WIDTH), jnp.float32),
        ),
        in_specs=[pl.BlockSpec(memory_space=pltpu.HBM)] * 4,
        out_specs=(vmem, vmem),
        scratch_shapes=scratch,
        compiler_params=pltpu.CompilerParams(
            collective_id=0, has_side_effects=True, vmem_limit_bytes=48 * 1024 * 1024
        ),
    )(*operands)


def per_device(features, labels, weights, sampled):
    loss, grad = head(features, labels.reshape(1, ROWS), weights, sampled)
    return (loss.reshape(ROWS), grad)


def solution(mesh):
    in_specs = (P(("cls", "dp"), None), P(("cls", "dp")), P("cls", None), P("cls"))
    out_specs = (P(("cls", "dp")), P(("cls", "dp"), None))
    return jax.shard_map(
        per_device, mesh=mesh, in_specs=in_specs, out_specs=out_specs, check_vma=False
    )
```

```python
import functools

import jax
import jax.numpy as jnp
from jax import lax
from jax.experimental import pallas as pl
from jax.experimental.pallas import tpu as pltpu
from jax.sharding import PartitionSpec as P

logit_scale = 64.0
margin = 0.35
epsilon = 1e-06

NX, NZ, NYH, NYL, NCORE = 4, 8, 2, 4, 2
ROWS = 128
OUT_ROWS = 32
BANK = 1024
WIDTH = 512
PAIR = 2 * ROWS
HALF = ROWS // 2
QUARTER = ROWS // 4
BANKS = NX * ROWS
EAST = 384
NORTH = WIDTH - EAST
EAST_CUTS = ((0, 256), (256, 128))


def normalize_rows(matrix):
    squares = jnp.sum(matrix * matrix, axis=1, keepdims=True)
    return lax.rsqrt(squares + epsilon)


def head_kernel(
    feat_ref,
    label_ref,
    bank_ref,
    sampled_ref,
    loss_ref,
    grad_ref,
    feats,
    classes,
    labels,
    ids,
    probs,
    grads,
    inverse_total,
    sums,
    sums_in,
    targets,
    targets_in,
    part_out,
    part_in,
    part_own,
    half_out,
    half_own,
    half_in,
    north_out,
    north_own,
    north_in,
    last_out,
    last_in,
    feat_in,
    places,
    bank,
    chosen,
    load_sem,
    feat_send,
    feat_recv,
    core_send,
    core_recv,
    label_send,
    label_recv,
    class_send,
    class_recv,
    sum_send,
    sum_recv,
    target_send,
    target_recv,
    part_send,
    part_recv,
    half_send,
    half_recv,
    north_send,
    north_recv,
    last_send,
    last_recv,
):
    cls, dp = lax.axis_index("cls"), lax.axis_index("dp")
    x, z, yh = lax.div(cls, 16), lax.rem(lax.div(cls, 2), 8), lax.rem(cls, 2)
    yl, core = lax.div(dp, 2), lax.rem(dp, 2)

    def device(dx=0, dz=0, dyh=0, dyl=0, dcore=0):
        px = lax.rem(x + dx, NX)
        pz = lax.rem(z + dz, NZ)
        pyh = lax.rem(yh + dyh, NYH)
        pyl = lax.rem(yl + dyl, NYL)
        pcore = lax.rem(core + dcore, NCORE)
        return ((px * NZ + pz) * NYH + pyh, pyl * NCORE + pcore)

    mirror = ((x * NZ + z) * NYH + (1 - yh), (NYL - 1 - yl) * NCORE + core)

    def copy(src, dst, send, recv, target):
        return pltpu.make_async_remote_copy(
            src_ref=src,
            dst_ref=dst,
            send_sem=send,
            recv_sem=recv,
            device_id=target,
            device_id_type=pl.DeviceIdType.MESH,
        )

    plane = [(o, w) for o in range(NZ) for w in range(NCORE) if (o, w) != (0, 0)]
    column = [(u, v) for u in range(NYH) for v in range(NYL) if (u, v) != (0, 0)]

    feat_load = pltpu.make_async_copy(feat_ref, feat_in, load_sem.at[0])
    label_load = pltpu.make_async_copy(label_ref, labels.at[0], load_sem.at[1])
    sampled_load = pltpu.make_async_copy(sampled_ref, places, load_sem.at[2])
    bank_load = pltpu.make_async_copy(bank_ref, bank, load_sem.at[3])
    for one in (feat_load, label_load, sampled_load, bank_load):
        one.start()
    barrier = pltpu.get_barrier_semaphore()
    peers = [device(dz=o, dcore=w) for o, w in plane]
    peers += [device(dx=i) for i in range(1, NX)]
    peers += [device(dyh=u, dyl=v) for u, v in column]
    for peer in peers:
        pl.semaphore_signal(barrier, inc=1, device_id=peer, device_id_type=pl.DeviceIdType.MESH)
    feat_load.wait()
    feat_wide = feat_in[...].astype(jnp.float32)
    feats[0, :ROWS] = (feat_wide * normalize_rows(feat_wide)).astype(jnp.bfloat16)
    label_load.wait()
    sums[...] = jnp.zeros_like(sums)
    targets[...] = jnp.zeros_like(targets)
    pl.semaphore_wait(barrier, len(peers))

    def feat_copy(slot, h):
        if slot < NZ // 2 or (slot == NZ // 2 and h < 2):
            came, target = slot - 1, device(dz=1)
        else:
            came, target = (slot + 1) % NZ, device(dz=NZ - 1)
        rows = pl.ds(h * QUARTER, QUARTER)
        k = 4 * slot + h
        return copy(
            feats.at[came, rows], feats.at[slot, rows], feat_send.at[k], feat_recv.at[k], target
        )

    def core_copy(slot, h):
        rows = pl.ds(h * HALF, HALF)
        k = 2 * slot + h
        return copy(
            feats.at[slot, rows],
            feats.at[slot, pl.ds(ROWS + h * HALF, HALF)],
            core_send.at[k],
            core_recv.at[k],
            device(dcore=1),
        )

    def class_copy(i, u, h):
        rows = pl.ds(i * ROWS + h * HALF, HALF)
        near = pl.ds(h * HALF, HALF)
        if i == 0:
            target = mirror
        else:
            target = device(dx=i)
        k = 4 * i + 2 * u + h
        src = classes.at[1 if i and u else 0, near]
        return copy(src, classes.at[u, rows], class_send.at[k], class_recv.at[k], target)

    def label_copy(o, w):
        k = 2 * o + w
        return copy(
            labels.at[0], labels.at[k], label_send.at[k], label_recv.at[k], device(dz=o, dcore=w)
        )

    feat_copies = {(s, h): feat_copy(s, h) for s in range(1, NZ) for h in range(4)}
    core_copies = {(s, h): core_copy(s, h) for s in range(NZ) for h in range(2)}
    class_copies = {
        (i, u, h): class_copy(i, u, h)
        for i in range(NX)
        for u in range(2)
        for h in range(2)
        if i + u
    }
    label_copies = [label_copy(o, w) for o, w in plane]

    for h in range(4):
        feat_copies[1, h].start()
        feat_copies[NZ - 1, h].start()
    for h in range(2):
        core_copies[0, h].start()
    for one in label_copies:
        one.start()

    sampled_load.wait()
    bank_load.wait()

    @pl.loop(0, ROWS // 8)
    def _(block):
        for r in range(8):
            k = block * 8 + r
            place = lax.div(k, OUT_ROWS) * (2 * OUT_ROWS) + core * OUT_ROWS + lax.rem(k, OUT_ROWS)
            chosen[pl.ds(k, 1)] = bank[pl.ds(places[place], 1)]

    picked = chosen[...]
    classes[0, :ROWS] = (picked * normalize_rows(picked)).astype(jnp.bfloat16)
    row = lax.broadcasted_iota(jnp.int32, (ROWS, PAIR), 0)
    within = (
        lax.shift_right_logical(row, 5) * (2 * OUT_ROWS)
        + lax.bitwise_and(row, OUT_ROWS - 1)
        + (z * (2 * PAIR) + core * OUT_ROWS)
    )
    for i in range(NX):
        base = lax.rem(x + (NX - i), NX) * (NZ * NYH * PAIR)
        ids[0, i * ROWS : (i + 1) * ROWS] = within + (base + yh * PAIR)
        ids[1, i * ROWS : (i + 1) * ROWS] = within + (base + (1 - yh) * PAIR)
    for h in range(2):
        class_copies[0, 1, h].start()
    for i in (2, 1, 3):
        for h in range(2):
            class_copies[i, 0, h].start()

    def names(s):
        return jnp.concatenate([labels[2 * s], labels[2 * s + 1]], axis=1)

    def first_pass(s, u):
        cosine = lax.dot_general(
            classes[u],
            feats[s],
            (((1,), (1,)), ((), ())),
            preferred_element_type=jnp.float32,
        )
        hit = ids[u] == names(s)
        logits = logit_scale * (cosine - jnp.where(hit, margin, 0.0))
        prob = jnp.exp(logits - logit_scale)
        probs[u, s] = prob
        total = jnp.sum(prob, axis=0, keepdims=True)
        target = jnp.sum(jnp.where(hit, logits, 0.0), axis=0, keepdims=True)
        sums[0, pl.ds(s, 1)] += total[:, :ROWS]
        sums[1, pl.ds(s, 1)] += total[:, ROWS:]
        targets[2 * s] += target[:, :ROWS]
        targets[2 * s + 1] += target[:, ROWS:]

    def forward_classes(h):
        class_copies[0, 1, h].wait_recv()
        for i in (2, 1, 3):
            class_copies[i, 1, h].start()

    def receive_features(step):
        back = NZ - step
        for h in range(4):
            if step < NZ // 2:
                feat_copies[step, h].wait_recv()
                if step + 1 < NZ // 2 or h < 2:
                    feat_copies[step + 1, h].start()
                feat_copies[back, h].wait_recv()
                if step + 1 < NZ // 2 or h >= 2:
                    feat_copies[back - 1, h].start()
                if h % 2:
                    core_copies[step, h // 2].start()
                    core_copies[back, h // 2].start()
            if step == 3 and h == 1:
                forward_classes(1)
        if step == NZ // 2:
            for h in (0, 2, 1, 3):
                feat_copies[step, h].wait_recv()
                if h in (1, 3):
                    core_copies[step, h // 2].start()

    def receive_cores(*slots):
        for slot in slots:
            for h in range(2):
                core_copies[slot, h].wait_recv()

    def receive_classes(u):
        for i in range(1, NX):
            for h in range(2):
                class_copies[i, u, h].wait_recv()

    receive_features(1)
    receive_features(2)
    forward_classes(0)
    receive_features(3)
    receive_classes(0)
    for one in label_copies:
        one.wait_recv()
    receive_cores(0, 1, 7)

    @pl.loop(0, 3)
    def _(k):
        first_pass(lax.rem(k + (NZ - 1), NZ), 0)

    receive_cores(2, 6, 3, 5)

    @pl.loop(0, 4)
    def _(k):
        first_pass(2 + lax.div(k, 2) + lax.rem(k, 2) * (NZ - 4 - 2 * lax.div(k, 2)), 0)

    receive_features(4)
    receive_classes(1)

    @pl.loop(0, 3)
    def _(k):
        first_pass(lax.rem(k + (NZ - 1), NZ), 1)

    @pl.loop(0, 4)
    def _(k):
        first_pass(2 + lax.div(k, 2) + lax.rem(k, 2) * (NZ - 4 - 2 * lax.div(k, 2)), 1)

    receive_cores(4)

    @pl.loop(0, 2)
    def _(k):
        first_pass(NZ // 2, k)

    sum_copies, target_copies = {}, {}
    for o, w in plane:
        k = 2 * o + w
        sum_copies[o, w] = copy(
            sums, sums_in.at[k], sum_send.at[k], sum_recv.at[k], device(dz=o, dcore=w)
        )
        target_copies[o, w] = copy(
            targets.at[k],
            targets_in.at[k],
            target_send.at[k],
            target_recv.at[k],
            device(dz=NZ - o, dcore=w),
        )
    for one in sum_copies.values():
        one.start()
    for one in target_copies.values():
        one.start()
    whole = [sums[0], sums[1]]
    for (o, w), one in sum_copies.items():
        one.wait_recv()
        for q in range(2):
            other = sums_in[2 * o + w, (q + w) % 2]
            whole[q] += other if o == 0 else pltpu.roll(other, o, 0)
    for q in range(2):
        inverse_total[q] = 1.0 / whole[q]

    part_copies, north_copies = {}, {}

    def send_part(turn, i):
        columns = pl.ds(*EAST_CUTS[turn])
        part_copies[turn, i] = copy(
            part_out.at[i, :, columns],
            part_in.at[i, :, columns],
            part_send.at[NX * turn + i],
            part_recv.at[NX * turn + i],
            device(dx=NX - i),
        )
        part_copies[turn, i].start()

    for i in (2, 1, 3, 0):

        def weigh(s, carry):
            inverse = jnp.concatenate(
                [inverse_total[0, pl.ds(s, 1)], inverse_total[1, pl.ds(s, 1)]], axis=1
            )
            name = names(s)
            for u in range(2):
                rows = pl.ds(i * ROWS, ROWS)
                hit = jnp.where(ids[u, rows] == name, 1.0, 0.0)
                slope = probs[u, s, rows] * inverse - hit
                grads[s, u * ROWS : (u + 1) * ROWS] = slope.astype(jnp.bfloat16)
            return carry

        lax.fori_loop(0, NZ, weigh, 0)
        part = jnp.zeros((PAIR, WIDTH), jnp.float32)
        for s in range(NZ):
            part += jnp.dot(grads[s], feats[s], preferred_element_type=jnp.float32)
        north = part[:, EAST:].reshape(NYH * NYL, OUT_ROWS, NORTH)
        north_own[i] = north
        north_out[i] = north.astype(jnp.bfloat16)
        if i == 0:
            part_own[...] = part[:, :EAST]
        else:
            part_out[i] = part[:, :EAST].astype(jnp.bfloat16)
            send_part(0, i)
        for u, v in column:
            k = NYL * u + v
            north_copies[i, k] = copy(
                north_out.at[i, NYL * u + lax.rem(yl + v, NYL)],
                north_in.at[i, k],
                north_send.at[NX * k + i],
                north_recv.at[NX * k + i],
                device(dyh=u, dyl=v),
            )
            north_copies[i, k].start()

    for i in (2, 1, 3):
        send_part(1, i)

    own_target = targets[0]
    for (o, w), one in target_copies.items():
        one.wait_recv()
        own_target += targets_in[2 * o + w]
    loss_ref[...] = logit_scale + jnp.log(whole[0][0:1]) - own_target

    last_copies = {}
    for i in (2, 1, 3, 0):
        north = north_own[i, yl]
        for k in range(1, NYH * NYL):
            north_copies[i, k].wait_recv()
            north += north_in[i, k].astype(jnp.float32)
        if i > 0:
            last_out[i] = north.astype(jnp.bfloat16)
            last_copies[i] = copy(
                last_out.at[i],
                last_in.at[i],
                last_send.at[i],
                last_recv.at[i],
                device(dx=NX - i),
            )
            last_copies[i].start()

    half_copies = {}
    for turn, (start, width) in enumerate(EAST_CUTS):
        columns = slice(start, start + width)
        half = part_own[:, columns]
        for i in (1, 3, 2):
            part_copies[turn, i].wait_recv()
            half += part_in[i, :, columns].astype(jnp.float32)
        half = half.reshape(NYH * NYL, OUT_ROWS, width)
        half_own[:, :, columns] = half
        half_out[:, :, columns] = half.astype(jnp.bfloat16)
        for u, v in column:
            k = NYL * u + v
            half_copies[turn, k] = copy(
                half_out.at[NYL * u + lax.rem(yl + v, NYL), :, pl.ds(start, width)],
                half_in.at[k, :, pl.ds(start, width)],
                half_send.at[NYH * NYL * turn + k],
                half_recv.at[NYH * NYL * turn + k],
                device(dyh=u, dyl=v),
            )
            half_copies[turn, k].start()
    for i, one in last_copies.items():
        one.wait_recv()
        north += last_in[i].astype(jnp.float32)
    pieces = []
    for turn, (start, width) in enumerate(EAST_CUTS):
        columns = slice(start, start + width)
        piece = half_own[yl, :, columns]
        for k in range(1, NYH * NYL):
            half_copies[turn, k].wait_recv()
            piece += half_in[k, :, columns].astype(jnp.float32)
        pieces.append(piece)
    pieces.append(north)
    total = (logit_scale / 8.0) * jnp.concatenate(pieces, axis=1)
    own = chosen[pl.ds(pl.multiple_of(yl * OUT_ROWS, OUT_ROWS), OUT_ROWS)]
    inverse = normalize_rows(own)
    unit = own * inverse
    radial = jnp.sum(unit * total, axis=1, keepdims=True)
    grad_ref[...] = inverse * (total - unit * radial)

    for group in (
        feat_copies,
        core_copies,
        class_copies,
        sum_copies,
        target_copies,
        part_copies,
        half_copies,
        north_copies,
        last_copies,
    ):
        for one in group.values():
            one.wait_send()
    for one in label_copies:
        one.wait_send()


def head(features, labels, weights, sampled):
    vmem = pl.BlockSpec(memory_space=pltpu.VMEM)
    operands = [
        pltpu.with_memory_space_constraint(one, pltpu.HBM)
        for one in (features, labels, weights, sampled)
    ]
    dma = pltpu.SemaphoreType.DMA
    slots, column = NZ * NCORE, NYH * NYL
    scratch = [
        pltpu.VMEM((NZ, PAIR, WIDTH), jnp.bfloat16),
        pltpu.VMEM((2, BANKS, WIDTH), jnp.bfloat16),
        pltpu.VMEM((slots, 1, ROWS), jnp.int32),
        pltpu.VMEM((2, BANKS, PAIR), jnp.int32),
        pltpu.VMEM((2, NZ, BANKS, PAIR), jnp.float32),
        pltpu.VMEM((NZ, PAIR, PAIR), jnp.bfloat16),
        pltpu.VMEM((2, NZ, ROWS), jnp.float32),
        pltpu.VMEM((2, NZ, ROWS), jnp.float32),
        pltpu.VMEM((slots, 2, NZ, ROWS), jnp.float32),
        pltpu.VMEM((slots, 1, ROWS), jnp.float32),
        pltpu.VMEM((slots, 1, ROWS), jnp.float32),
        pltpu.VMEM((NX, PAIR, EAST), jnp.bfloat16),
        pltpu.VMEM((NX, PAIR, EAST), jnp.bfloat16),
        pltpu.VMEM((PAIR, EAST), jnp.float32),
        pltpu.VMEM((column, OUT_ROWS, EAST), jnp.bfloat16),
        pltpu.VMEM((column, OUT_ROWS, EAST), jnp.float32),
        pltpu.VMEM((column, OUT_ROWS, EAST), jnp.bfloat16),
        pltpu.VMEM((NX, column, OUT_ROWS, NORTH), jnp.bfloat16),
        pltpu.VMEM((NX, column, OUT_ROWS, NORTH), jnp.float32),
        pltpu.VMEM((NX, column, OUT_ROWS, NORTH), jnp.bfloat16),
        pltpu.VMEM((NX, OUT_ROWS, NORTH), jnp.bfloat16),
        pltpu.VMEM((NX, OUT_ROWS, NORTH), jnp.bfloat16),
        pltpu.VMEM((ROWS, WIDTH), jnp.bfloat16),
        pltpu.SMEM((PAIR,), jnp.int32),
        pltpu.VMEM((BANK, WIDTH), jnp.float32),
        pltpu.VMEM((ROWS, WIDTH), jnp.float32),
        dma((4,)),
    ]
    counts = (4 * NZ, 2 * NZ, slots, 4 * NX, slots, slots, 2 * NX, 2 * column, NX * column, NX)
    for count in counts:
        scratch += [dma((count,)), dma((count,))]
    return pl.pallas_call(
        head_kernel,
        out_shape=(
            jax.ShapeDtypeStruct((1, ROWS), jnp.float32),
            jax.ShapeDtypeStruct((OUT_ROWS, WIDTH), jnp.float32),
        ),
        in_specs=[pl.BlockSpec(memory_space=pltpu.HBM)] * 4,
        out_specs=(vmem, vmem),
        scratch_shapes=scratch,
        compiler_params=pltpu.CompilerParams(
            collective_id=0, has_side_effects=True, vmem_limit_bytes=48 * 1024 * 1024
        ),
    )(*operands)


def per_device(features, labels, weights, sampled):
    loss, grad = head(features, labels.reshape(1, ROWS), weights, sampled)
    return (loss.reshape(ROWS), grad)


def solution(mesh):
    in_specs = (P(("cls", "dp"), None), P(("cls", "dp")), P("cls", None), P("cls"))
    out_specs = (P(("cls", "dp")), P(("cls", "dp"), None))
    return jax.shard_map(
        per_device, mesh=mesh, in_specs=in_specs, out_specs=out_specs, check_vma=False
    )
```
